512 devices in a mesh: seq: 128 (over z, y, core), tp: 4 (over x).
Axes of the slice: x: 4, y: 4, z: 16, core: 2. Of those that a mesh axis runs over, the one named last changes fastest.
Arguments:
- query_states: bfloat16 [8192, 4096], P('seq', 'tp'), may hold values from -384 to 384
- key_states: bfloat16 [8192, 4096], P('seq', 'tp'), may hold values from -12 to 12
- value_states: bfloat16 [8192, 4096], P('seq', 'tp'), may hold values from -6 to 6
- residual: bfloat16 [8192, 4096], P('seq', 'tp'), may hold values from -3 to 3
- segment_ids: int32 [8192], replicated, may hold values from 0 to 7, never falling along the last dimension, each value on 1 to 4096 neighbouring positions
- positions: int32 [2, 8192], P(None, 'seq'), may hold values from 0 to 63
- out_weight: bfloat16 [4096, 4096], P('tp', 'seq'), may hold values from -0.375 to 0.375
- layer_scale: float32 [4096], P('tp'), may hold values from 0.5 to 2
Outputs:
- encoded: bfloat16 [8192, 4096], P('seq', 'tp')
The draws below stay inside these ranges and needn't reach their ends.
Inputs may be any that keep to these rules, and one draw needn't show every extreme that they name: `segment_ids`: the ids never fall along the row, and each id covers one run of at most 4096 positions.
All inputs are finite; a program needn't handle non-finite values.
Results may differ from the reference program's by a relative error of at most 0.0072.
Values may be sent and summed in bfloat16 or wider, within the bound.
A program may use at most 128 MiB of HBM per device.

```python
import math
import jax
import jax.numpy as jnp
import numpy as np
from jax import lax

H = 32
DH = 128
D = 4096
ROW_LEN = 8192
SEGS = 8


def paired_states(key):
    full_shape = (ROW_LEN, H * DH)
    key_base = jnp.clip(jax.random.normal(jax.random.fold_in(key, 11), full_shape, jnp.float32), -6.0, 6.0)
    query_base = jnp.clip(jax.random.normal(jax.random.fold_in(key, 12), full_shape, jnp.float32), -6.0, 6.0)
    return (query_base, key_base)


def draw_query_states(key, part):
    return paired_states(key)[0].astype(jnp.bfloat16)


def draw_key_states(key, part):
    return paired_states(key)[1].astype(jnp.bfloat16)


def plant(values, own_key, low, largest):
    longest = values.shape.index(max(values.shape))
    spots = []
    for shift in (0, 1):
        where = [jax.random.randint(jax.random.fold_in(own_key, axis), (), 0, length) for axis, length in enumerate(values.shape)]
        where[longest] = (where[longest] + shift) % values.shape[longest]
        spots.append(tuple(where))
    return values.at[spots[0]].set(low).at[spots[1]].set(largest)


def levels(key, dims, shards, low, top_value):
    gain, own = 1.0, jax.random.fold_in(key, 6)
    for dim, shards_of in shards:
        steps = jnp.exp(jax.random.uniform(jax.random.fold_in(own, dim), (shards_of,), jnp.float32, low / len(shards), top_value / len(shards)))
        gain = gain * jnp.repeat(steps, dims[dim] // shards_of).reshape([-1 if axis == dim else 1 for axis in range(len(dims))])
    return gain


def split_up(number_of, total, bound, lean):
    weights = [(1 << 20) // math.isqrt(grade ** lean) + 1 for grade in range(2, number_of + 1)]
    spare, holding = total - bound - (number_of - 1), [1] * (number_of - 1)
    while spare > 0:
        free = [i for i in range(number_of - 1) if holding[i] < bound]
        pool, left = sum([weights[i] for i in free]), spare
        for i in free:
            addition = min(bound - holding[i], max(1, left * weights[i] // pool), spare)
            holding[i] = holding[i] + addition
            spare = spare - addition
    return np.array([bound] + holding)


def uneven(stream_key, amount, total, reach, slope):
    if amount == 2:
        one = jax.random.randint(stream_key, (), max(1, total - reach), min(reach, total - 1) + 1)
        return jnp.stack([one, total - one])
    lengths = jnp.asarray(split_up(amount, total, reach, slope), jnp.int32)
    twos = (amount - 1) // 2
    donor, receiver = lengths[1:1 + 2 * twos:2], lengths[2:2 + 2 * twos:2]
    room = jnp.minimum(donor - 1, reach - receiver)
    moved = jax.random.randint(jax.random.fold_in(stream_key, 1), (twos,), 0, 1 << 20) % (room + 1)
    lengths = lengths.at[1:1 + 2 * twos:2].set(donor - moved).at[2:2 + 2 * twos:2].set(receiver + moved)
    return lengths[jax.random.permutation(jax.random.fold_in(stream_key, 2), amount)]


def centred(own_key, shape, deviation, most, pieces=(), held_as=jnp.bfloat16):
    drawn = jax.random.normal(own_key, shape, jnp.float32) * deviation
    if len(pieces) > 0:
        drawn = levels(own_key, shape, pieces, -0.22, 0.18) * drawn
    return jnp.clip(drawn, min=-most, max=most).astype(held_as)


def setup_inputs(seed: int = 0) -> dict:
    keys = jax.random.split(jax.random.key(seed), 9)
    query_states = draw_query_states(jax.random.fold_in(keys[8], 71), 0)
    key_states = draw_key_states(jax.random.fold_in(keys[8], 71), 0)
    value_states = centred(keys[2], (ROW_LEN, D), 1.0, 6.0, ((0, 128), (1, 4)))
    residual = centred(keys[3], (ROW_LEN, D), 0.5, 3.0, ((0, 128), (1, 4)))
    segment_ids = jnp.searchsorted(jnp.cumsum(uneven(keys[4], SEGS, ROW_LEN, ROW_LEN // 2, 2)), jnp.arange(ROW_LEN), side="right").astype(jnp.int32)
    positions = plant(jax.random.randint(keys[5], (2, ROW_LEN), 0, 64), jax.random.fold_in(keys[5], 1), 0, 63).astype(jnp.int32)
    out_weight = centred(keys[6], (D, D), (D // 16) ** -0.5, 0.375, ((0, 4), (1, 128)))
    layer_scale = jnp.clip(jnp.exp(math.log(2.0) - 1.3862944 * jax.random.uniform(keys[7], (D,), jnp.float32) ** levels(keys[7], (D,), ((0, 4),), -0.2, 0.2)), 0.5, 2.0)
    return dict(query_states=query_states, key_states=key_states, value_states=value_states, residual=residual, segment_ids=segment_ids, positions=positions, out_weight=out_weight, layer_scale=layer_scale)


masked_score = -1e30


def rotary(states, positions):
    quarter = DH // 4
    frequency = 100.0 ** (-jnp.arange(quarter, dtype=jnp.float32) / quarter)
    angles = positions.astype(jnp.float32)[:, :, None] * frequency
    angles = jnp.moveaxis(angles, 0, 1)
    cosine = jnp.cos(angles)[:, None, :, None, :]
    sine_table = jnp.sin(angles)[:, None, :, None, :]
    local_span, feature_width = states.shape
    shaped = states.reshape(local_span, feature_width // DH, 2, 2, quarter)
    partner = jnp.flip(shaped, axis=3)
    signed = jnp.array([-1.0, 1.0], jnp.float32)[:, None]
    rotated = shaped * cosine + partner * sine_table * signed
    return rotated.reshape(local_span, feature_width)


def attend_block(query_block, query_segments, key_item, value_item, segment_row):
    scores = jnp.dot(query_block, key_item.T, preferred_element_type=jnp.float32) * (DH ** -0.5)
    allowed = query_segments[:, None] == segment_row[None, :]
    scores = jnp.where(allowed, scores, masked_score)
    row_peak = jnp.max(scores, axis=1, keepdims=True)
    exponent = jnp.exp(scores - row_peak)
    row_total = jnp.sum(exponent, axis=1, keepdims=True)
    weights = exponent.astype(jnp.bfloat16)
    weighted = jnp.dot(weights, value_item, preferred_element_type=jnp.float32)
    return (weighted / row_total).astype(jnp.bfloat16)


def reference(query_states, key_states, value_states, residual, segment_ids, positions, out_weight, layer_scale):
    rotated_q = rotary(query_states.astype(jnp.float32), positions).astype(jnp.bfloat16)
    rotated_k = rotary(key_states.astype(jnp.float32), positions).astype(jnp.bfloat16)
    block_rows = min(512, ROW_LEN)
    block_count = ROW_LEN // block_rows
    segment_blocks = segment_ids.reshape(block_count, block_rows)

    def one_head(head_index):
        zero_index = jnp.zeros((), jnp.int32)
        column = (head_index * DH).astype(jnp.int32)
        query_item = lax.dynamic_slice(rotated_q, (zero_index, column), (ROW_LEN, DH))
        key_item = lax.dynamic_slice(rotated_k, (zero_index, column), (ROW_LEN, DH))
        value_item = lax.dynamic_slice(value_states, (zero_index, column), (ROW_LEN, DH))
        query_blocks = query_item.reshape(block_count, block_rows, DH)

        def one_block(pair):
            return attend_block(pair[0], pair[1], key_item, value_item, segment_ids)

        return lax.map(one_block, (query_blocks, segment_blocks)).reshape(ROW_LEN, DH)

    attended = lax.map(one_head, jnp.arange(H, dtype=jnp.int32))
    attended = attended.transpose(1, 0, 2).reshape(ROW_LEN, H * DH)
    projected = jnp.dot(attended, out_weight, preferred_element_type=jnp.float32)
    encoded = residual.astype(jnp.float32) + layer_scale * projected
    return encoded.astype(jnp.bfloat16)
```

```python
import functools
import math

import jax
import jax.numpy as jnp
import numpy as np
from jax import lax
from jax.experimental import pallas as pl
from jax.experimental.pallas import tpu as pltpu
from jax.sharding import PartitionSpec as P

DH = 128
PLANES = 16
LANES = 8
HALVES = 2
PIECE = 32
QUERY_ROWS = 128

masked_score = -1e30


def rotary(states, positions):
    quarter = DH // 4
    frequency = 100.0 ** (-jnp.arange(quarter, dtype=jnp.float32) / quarter)
    angles = positions.astype(jnp.float32)[:, :, None] * frequency
    angles = jnp.moveaxis(angles, 0, 1)
    cosine = jnp.cos(angles)[:, None, :, None, :]
    sine_table = jnp.sin(angles)[:, None, :, None, :]
    local_span, feature_width = states.shape
    shaped = states.reshape(local_span, feature_width // DH, 2, 2, quarter)
    partner = jnp.flip(shaped, axis=3)
    signed = jnp.array([-1.0, 1.0], jnp.float32)[:, None]
    rotated = shaped * cosine + partner * sine_table * signed
    return rotated.reshape(local_span, feature_width)


def attend_kernel(low_ref, high_ref, q_ref, kv_ref, qseg_ref, kseg_ref, out_ref, score_ref):
    scale = DH ** (-0.5) * math.log2(math.e)
    members = kv_ref.shape[0]
    keys = members * PIECE
    for tile in range(q_ref.shape[0] // QUERY_ROWS):
        rows = pl.ds(tile * QUERY_ROWS, QUERY_ROWS)
        query = q_ref[rows, :]
        query_segment = qseg_ref[rows, :]
        low, high = low_ref[tile], high_ref[tile]

        def score_step(plane, peak):
            start = pl.multiple_of(plane * PIECE, PIECE)
            key = kv_ref[:, 0, pl.ds(start, PIECE), :].reshape(keys, DH)
            score = lax.dot_general(
                query, key, (((1,), (1,)), ((), ())), preferred_element_type=jnp.float32
            )
            score = jnp.where(query_segment == kseg_ref[plane], score, masked_score)
            score_ref[plane] = score
            for part in range(keys // DH):
                peak = jnp.maximum(peak, score[:, part * DH:(part + 1) * DH])
            return peak

        peak = lax.fori_loop(
            low, high, score_step, jnp.full((QUERY_ROWS, DH), masked_score, jnp.float32)
        )
        peak = jnp.max(peak, axis=1, keepdims=True)

        def value_step(plane, carry):
            total, weighted = carry
            start = pl.multiple_of(plane * PIECE, PIECE)
            value = kv_ref[:, 1, pl.ds(start, PIECE), :].reshape(keys, DH)
            exponent = jnp.exp2((score_ref[plane] - peak) * scale)
            for part in range(keys // DH):
                total = total + exponent[:, part * DH:(part + 1) * DH]
            weighted = weighted + jnp.dot(
                exponent.astype(jnp.bfloat16), value, preferred_element_type=jnp.float32
            )
            return total, weighted

        zero = jnp.zeros((QUERY_ROWS, DH), jnp.float32)
        total, weighted = lax.fori_loop(low, high, value_step, (zero, zero))
        total = jnp.sum(total, axis=1, keepdims=True)
        out_ref[rows, :] = (weighted / total).astype(out_ref.dtype)


def attend(query, key_value, query_segment, key_segment, low, high):
    smem = pl.BlockSpec(memory_space=pltpu.SMEM)
    vmem = pl.BlockSpec(memory_space=pltpu.VMEM)
    keys = key_value.shape[0] * PIECE
    return pl.pallas_call(
        attend_kernel,
        out_shape=jax.ShapeDtypeStruct(query.shape, jnp.bfloat16),
        in_specs=[smem, smem, vmem, vmem, vmem, vmem],
        out_specs=vmem,
        scratch_shapes=[pltpu.VMEM((PLANES, QUERY_ROWS, keys), jnp.float32)],
        compiler_params=pltpu.CompilerParams(vmem_limit_bytes=40 * 1024 * 1024),
        cost_estimate=pl.CostEstimate(
            flops=4 * query.shape[0] * keys * PLANES * DH // 2,
            bytes_accessed=key_value.size * 2,
            transcendentals=query.shape[0] * keys * PLANES // 2,
        ),
    )(low, high, query, key_value, query_segment, key_segment)


def local(
    query_states,
    key_states,
    value_states,
    residual,
    segment_ids,
    positions,
    out_weight,
    layer_scale,
):
    local_span, feature_width = query_states.shape
    heads = feature_width // DH
    seq_count = lax.axis_size("seq")
    tp_count = lax.axis_size("tp")
    members = seq_count // heads
    seq_here = lax.axis_index("seq")

    by_column = seq_count // tp_count
    moves = []
    for block in range(tp_count):
        for source in range(tp_count):
            for i in range(by_column):
                moves.append(
                    ((block * by_column + i) * tp_count + source, (source * by_column + i) * tp_count + block)
                )
    weight = lax.ppermute(out_weight.T, ("seq", "tp"), moves)
    weight = lax.all_gather(weight, "seq", axis=0, tiled=True)
    weight = weight.reshape(tp_count, feature_width, feature_width)

    rotated_q = rotary(query_states.astype(jnp.float32), positions).astype(jnp.bfloat16)
    rotated_k = rotary(key_states.astype(jnp.float32), positions).astype(jnp.bfloat16)

    def chunk(states):
        return states.reshape(HALVES, PIECE, heads, DH).transpose(2, 0, 1, 3)

    sent = jnp.stack([chunk(rotated_q), chunk(rotated_k), chunk(value_states)], axis=2)
    sent = sent.reshape(PLANES, 3, PIECE, DH)
    rings = [[z * LANES + lane for z in range(PLANES)] for lane in range(LANES)]
    got = lax.all_to_all(sent, "seq", 0, 0, tiled=True, axis_index_groups=rings)
    query = got[:, 0].reshape(PLANES * PIECE, DH)
    key_value = got[:, 1:].transpose(1, 0, 2, 3).reshape(2, PLANES * PIECE, DH)
    squads = [[h * members + m for m in range(members)] for h in range(heads)]
    key_value = lax.all_gather(key_value, "seq", axis_index_groups=squads)

    grid = segment_ids.reshape(PLANES, LANES, HALVES, PIECE)
    key_segment = grid.transpose(0, 2, 1, 3).reshape(PLANES, 1, members * PIECE)
    half_here = (seq_here // LANES) % HALVES
    lane_here = seq_here % LANES
    query_segment = lax.dynamic_slice(
        grid, (0, lane_here, half_here, 0), (PLANES, 1, 1, PIECE)
    ).reshape(PLANES * PIECE)
    ends = query_segment.reshape(-1, QUERY_ROWS)
    plane_span = LANES * HALVES * PIECE
    low = jnp.sum(segment_ids[None, :] < ends[:, :1], axis=1, dtype=jnp.int32) // plane_span
    high = (
        jnp.sum(segment_ids[None, :] <= ends[:, -1:], axis=1, dtype=jnp.int32) + plane_span - 1
    ) // plane_span

    attended = attend(query, key_value, query_segment[:, None], key_segment, low, high)
    returned = lax.all_to_all(
        attended.reshape(PLANES, PIECE, DH), "seq", 0, 0, tiled=True, axis_index_groups=rings
    )
    returned = returned.reshape(heads, HALVES, PIECE, DH).transpose(1, 2, 0, 3)
    returned = returned.reshape(local_span, feature_width)
    gathered = lax.all_gather(returned, "tp")
    projected = lax.dot_general(
        gathered, weight, (((0, 2), (0, 2)), ((), ())), preferred_element_type=jnp.float32
    )
    encoded = residual.astype(jnp.float32) + layer_scale * projected
    return encoded.astype(jnp.bfloat16)


def solution(mesh):
    in_specs = (
        P("seq", "tp"),
        P("seq", "tp"),
        P("seq", "tp"),
        P("seq", "tp"),
        P(),
        P(None, "seq"),
        P("tp", "seq"),
        P("tp"),
    )
    out_specs = P("seq", "tp")
    return jax.shard_map(local, mesh=mesh, in_specs=in_specs, out_specs=out_specs, check_vma=False)
```

```python
import math

import jax
import jax.numpy as jnp
from jax import lax
from jax.experimental import pallas as pl
from jax.experimental.pallas import tpu as pltpu
from jax.sharding import PartitionSpec as P

DH = 128
PLANES = 16
LANES = 8
HALVES = 2
PIECE = 32
QUERY_ROWS = 128

MESH = pl.DeviceIdType.MESH

masked_score = -1e30


def rotary(states, positions):
    quarter = DH // 4
    frequency = 100.0 ** (-jnp.arange(quarter, dtype=jnp.float32) / quarter)
    angles = positions.astype(jnp.float32)[:, :, None] * frequency
    angles = jnp.moveaxis(angles, 0, 1)
    cosine = jnp.cos(angles)[:, None, :, None, :]
    sine_table = jnp.sin(angles)[:, None, :, None, :]
    local_span, feature_width = states.shape
    shaped = states.reshape(local_span, feature_width // DH, 2, 2, quarter)
    partner = jnp.flip(shaped, axis=3)
    signed = jnp.array([-1.0, 1.0], jnp.float32)[:, None]
    rotated = shaped * cosine + partner * sine_table * signed
    return rotated.reshape(local_span, feature_width)


def attend_kernel(low_ref, high_ref, q_ref, kv_ref, qseg_ref, kseg_ref, out_ref, score_ref):
    scale = DH ** (-0.5) * math.log2(math.e)
    members = kv_ref.shape[0]
    keys = members * PIECE
    for tile in range(q_ref.shape[0] // QUERY_ROWS):
        rows = pl.ds(tile * QUERY_ROWS, QUERY_ROWS)
        query = q_ref[rows, :]
        query_segment = qseg_ref[rows, :]
        low, high = low_ref[tile], high_ref[tile]

        def score_step(plane, peak):
            start = pl.multiple_of(plane * PIECE, PIECE)
            key = kv_ref[:, 0, pl.ds(start, PIECE), :].reshape(keys, DH)
            score = lax.dot_general(
                query, key, (((1,), (1,)), ((), ())), preferred_element_type=jnp.float32
            )
            score = jnp.where(query_segment == kseg_ref[plane], score, masked_score)
            score_ref[plane] = score
            for part in range(keys // DH):
                peak = jnp.maximum(peak, score[:, part * DH:(part + 1) * DH])
            return peak

        peak = lax.fori_loop(
            low, high, score_step, jnp.full((QUERY_ROWS, DH), masked_score, jnp.float32)
        )
        peak = jnp.max(peak, axis=1, keepdims=True)

        def value_step(plane, carry):
            total, weighted = carry
            start = pl.multiple_of(plane * PIECE, PIECE)
            value = kv_ref[:, 1, pl.ds(start, PIECE), :].reshape(keys, DH)
            exponent = jnp.exp2((score_ref[plane] - peak) * scale)
            for part in range(keys // DH):
                total = total + exponent[:, part * DH:(part + 1) * DH]
            weighted = weighted + jnp.dot(
                exponent.astype(jnp.bfloat16), value, preferred_element_type=jnp.float32
            )
            return total, weighted

        zero = jnp.zeros((QUERY_ROWS, DH), jnp.float32)
        total, weighted = lax.fori_loop(low, high, value_step, (zero, zero))
        total = jnp.sum(total, axis=1, keepdims=True)
        out_ref[rows, :] = (weighted / total).astype(out_ref.dtype)


def attend(query, key_value, query_segment, key_segment, low, high):
    smem = pl.BlockSpec(memory_space=pltpu.SMEM)
    vmem = pl.BlockSpec(memory_space=pltpu.VMEM)
    keys = key_value.shape[0] * PIECE
    return pl.pallas_call(
        attend_kernel,
        out_shape=jax.ShapeDtypeStruct(query.shape, jnp.bfloat16),
        in_specs=[smem, smem, vmem, vmem, vmem, vmem],
        out_specs=vmem,
        scratch_shapes=[pltpu.VMEM((PLANES, QUERY_ROWS, keys), jnp.float32)],
        compiler_params=pltpu.CompilerParams(vmem_limit_bytes=40 * 1024 * 1024),
        cost_estimate=pl.CostEstimate(
            flops=4 * query.shape[0] * keys * PLANES * DH // 2,
            bytes_accessed=key_value.size * 2,
            transcendentals=query.shape[0] * keys * PLANES // 2,
        ),
    )(low, high, query, key_value, query_segment, key_segment)


def finish_kernel(
    attended_ref,
    weight_ref,
    residual_ref,
    gain_ref,
    encoded_ref,
    plane_buf,
    part_buf,
    share_buf,
    z_send,
    z_recv,
    lane_send,
    lane_recv,
    share_send,
    share_recv,
):
    seq_here, tp_here = lax.axis_index("seq"), lax.axis_index("tp")
    z, lane = seq_here // LANES, seq_here % LANES
    block = lane // 2
    feeds_itself = jnp.where(block == tp_here, 1, 0)

    def along_z(step):
        return (z + step) % PLANES

    def in_plane(step):
        return (lane + step) % LANES

    def z_copy(source, dest):
        return pltpu.make_async_remote_copy(
            src_ref=attended_ref.at[dest],
            dst_ref=plane_buf.at[lane, source],
            send_sem=z_send.at[dest],
            recv_sem=z_recv.at[source],
            device_id=(dest * LANES + lane, tp_here),
            device_id_type=MESH,
        )

    def lane_copy(source, dest):
        return pltpu.make_async_remote_copy(
            src_ref=plane_buf.at[source],
            dst_ref=plane_buf.at[source],
            send_sem=lane_send.at[dest],
            recv_sem=lane_recv.at[source],
            device_id=(z * LANES + dest, tp_here),
            device_id_type=MESH,
        )

    def share_copy(source, dest):
        return pltpu.make_async_remote_copy(
            src_ref=part_buf.at[dest],
            dst_ref=share_buf.at[source],
            send_sem=share_send.at[dest],
            recv_sem=share_recv.at[source],
            device_id=(z * LANES + dest, block),
            device_id_type=MESH,
        )

    def each(start, stop, act):
        def body(step, carry):
            act(step)
            return carry

        lax.fori_loop(start, stop, body, 0)

    barrier = pltpu.get_barrier_semaphore()

    def greet(seq, tp):
        pl.semaphore_signal(barrier, inc=1, device_id=(seq, tp), device_id_type=MESH)

    each(1, PLANES, lambda step: greet(along_z(step) * LANES + lane, tp_here))
    each(1, LANES, lambda step: greet(z * LANES + in_plane(step), tp_here))

    def greet_feeder(source):
        feeder_tp, feeder_lane = source // 2, 2 * tp_here + source % 2

        @pl.when(jnp.logical_or(feeder_tp != tp_here, feeder_lane != lane))
        def _():
            greet(z * LANES + feeder_lane, feeder_tp)

    each(0, LANES, greet_feeder)
    pl.semaphore_wait(barrier, PLANES - 1 + LANES - 1 + LANES - feeds_itself)

    each(1, PLANES, lambda step: z_copy(z, along_z(step)).start())
    plane_buf[lane, z] = attended_ref[z]
    each(1, PLANES, lambda step: z_copy(along_z(step), z).wait_recv())

    each(1, LANES, lambda step: lane_copy(lane, in_plane(step)).start())
    each(1, LANES, lambda step: lane_copy(in_plane(step), lane).wait_recv())

    per_step = 4
    heads = PLANES // HALVES
    rows = per_step * HALVES * PIECE
    for step in range(LANES // per_step):
        token = plane_buf[step * per_step:(step + 1) * per_step]
        token = jnp.concatenate(
            [token[:, HALVES * h:HALVES * (h + 1)].reshape(rows, DH) for h in range(heads)], axis=1
        )
        part = lax.dot_general(
            token, weight_ref[...], (((1,), (1,)), ((), ())), preferred_element_type=jnp.float32
        )
        part_buf[step * per_step:(step + 1) * per_step] = part.astype(jnp.bfloat16).reshape(
            per_step, HALVES * PIECE, part.shape[1]
        )

    own_source = tp_here * 2 + lane % 2

    def share_out(step):
        dest = in_plane(step)

        @pl.when(jnp.logical_or(block != tp_here, dest != lane))
        def _():
            share_copy(own_source, dest).start()

        @pl.when(jnp.logical_and(block == tp_here, dest == lane))
        def _():
            share_buf[own_source] = part_buf[dest]

    each(0, LANES, share_out)

    def collect(source):
        feeder_tp, feeder_lane = source // 2, 2 * tp_here + source % 2

        @pl.when(jnp.logical_or(feeder_tp != tp_here, feeder_lane != lane))
        def _():
            share_copy(source, lane).wait_recv()

    each(0, LANES, collect)
    width = part_buf.shape[2]
    for half in range(2):
        columns = slice(half * width, (half + 1) * width)
        total = share_buf[half].astype(jnp.float32)
        for source in range(1, LANES // 2):
            total = total + share_buf[2 * source + half].astype(jnp.float32)
        encoded = residual_ref[:, columns].astype(jnp.float32) + gain_ref[:, columns] * total
        encoded_ref[:, columns] = encoded.astype(encoded_ref.dtype)

    each(1, PLANES, lambda step: z_copy(z, along_z(step)).wait_send())
    each(1, LANES, lambda step: lane_copy(lane, in_plane(step)).wait_send())

    def share_sent(step):
        dest = in_plane(step)

        @pl.when(jnp.logical_or(block != tp_here, dest != lane))
        def _():
            share_copy(own_source, dest).wait_send()

    each(0, LANES, share_sent)


def finish(attended, weight, residual, gain):
    vmem = pl.BlockSpec(memory_space=pltpu.VMEM)
    return pl.pallas_call(
        finish_kernel,
        out_shape=jax.ShapeDtypeStruct(residual.shape, jnp.bfloat16),
        in_specs=[vmem] * 4,
        out_specs=vmem,
        scratch_shapes=[
            pltpu.VMEM((LANES, PLANES, PIECE, DH), jnp.bfloat16),
            pltpu.VMEM((LANES, HALVES * PIECE, weight.shape[0]), jnp.bfloat16),
            pltpu.VMEM((LANES, HALVES * PIECE, weight.shape[0]), jnp.bfloat16),
            pltpu.SemaphoreType.DMA((PLANES,)),
            pltpu.SemaphoreType.DMA((PLANES,)),
            pltpu.SemaphoreType.DMA((LANES,)),
            pltpu.SemaphoreType.DMA((LANES,)),
            pltpu.SemaphoreType.DMA((LANES,)),
            pltpu.SemaphoreType.DMA((LANES,)),
        ],
        compiler_params=pltpu.CompilerParams(
            collective_id=1, has_side_effects=True, vmem_limit_bytes=32 * 1024 * 1024
        ),
    )(attended, weight, residual, gain)


def local(
    query_states,
    key_states,
    value_states,
    residual,
    segment_ids,
    positions,
    out_weight,
    layer_scale,
):
    local_span, feature_width = query_states.shape
    heads = feature_width // DH
    seq_count = lax.axis_size("seq")
    members = seq_count // heads
    seq_here = lax.axis_index("seq")

    rings = [[z * LANES + lane for z in range(PLANES)] for lane in range(LANES)]
    moves = [
        (lane * PLANES + z, z * LANES + lane) for lane in range(LANES) for z in range(PLANES)
    ]
    weight = lax.ppermute(out_weight.T, "seq", moves)
    weight = lax.all_gather(weight, "seq", axis_index_groups=rings, axis=0, tiled=True)

    rotated_q = rotary(query_states.astype(jnp.float32), positions).astype(jnp.bfloat16)
    rotated_k = rotary(key_states.astype(jnp.float32), positions).astype(jnp.bfloat16)

    def chunk(states):
        return states.reshape(HALVES, PIECE, heads, DH).transpose(2, 0, 1, 3)

    sent = jnp.stack([chunk(rotated_q), chunk(rotated_k), chunk(value_states)], axis=2)
    sent = sent.reshape(PLANES, 3, PIECE, DH)
    got = lax.all_to_all(sent, "seq", 0, 0, tiled=True, axis_index_groups=rings)
    query = got[:, 0].reshape(PLANES * PIECE, DH)
    key_value = got[:, 1:].transpose(1, 0, 2, 3).reshape(2, PLANES * PIECE, DH)
    squads = [[h * members + m for m in range(members)] for h in range(heads)]
    key_value = lax.all_gather(key_value, "seq", axis_index_groups=squads)

    grid = segment_ids.reshape(PLANES, LANES, HALVES, PIECE)
    key_segment = grid.transpose(0, 2, 1, 3).reshape(PLANES, 1, members * PIECE)
    half_here = (seq_here // LANES) % HALVES
    lane_here = seq_here % LANES
    query_segment = lax.dynamic_slice(
        grid, (0, lane_here, half_here, 0), (PLANES, 1, 1, PIECE)
    ).reshape(PLANES * PIECE)
    ends = query_segment.reshape(-1, QUERY_ROWS)
    plane_span = LANES * HALVES * PIECE
    low = jnp.sum(segment_ids[None, :] < ends[:, :1], axis=1, dtype=jnp.int32) // plane_span
    high = (
        jnp.sum(segment_ids[None, :] <= ends[:, -1:], axis=1, dtype=jnp.int32) + plane_span - 1
    ) // plane_span

    attended = attend(query, key_value, query_segment[:, None], key_segment, low, high)
    return finish(
        attended.reshape(PLANES, PIECE, DH), weight, residual, layer_scale[None, :]
    )


def solution(mesh):
    in_specs = (
        P("seq", "tp"),
        P("seq", "tp"),
        P("seq", "tp"),
        P("seq", "tp"),
        P(),
        P(None, "seq"),
        P("tp", "seq"),
        P("tp"),
    )
    out_specs = P("seq", "tp")
    return jax.shard_map(local, mesh=mesh, in_specs=in_specs, out_specs=out_specs, check_vma=False)
```

```python
import math

import jax
import jax.numpy as jnp
from jax import lax
from jax.experimental import pallas as pl
from jax.experimental.pallas import tpu as pltpu
from jax.sharding import PartitionSpec as P

DH = 128
PLANES = 16
LANES = 8
GROUPS = 4
SPAN = 64
TOKENS = LANES * SPAN
CHUNK = 128
HALF_RING = PLANES // 2
EXPONENT_SCALE = DH ** (-0.5) * math.log2(math.e)
MESH = pl.DeviceIdType.MESH

masked_score = -1e30


def each(start, stop, act):
    def body(step, carry):
        act(step)
        return carry

    lax.fori_loop(start, stop, body, 0)


def layer_kernel(
    query_ref,
    key_ref,
    value_ref,
    residual_ref,
    segment_ref,
    position_ref,
    weight_ref,
    gain_ref,
    encoded_ref,
    send_buf,
    stage_buf,
    kv_buf,
    weight_buf,
    query_segment,
    peak_ref,
    total_ref,
    sum_ref,
    plane_buf,
    part_buf,
    share_buf,
    stage_send,
    stage_recv,
    ring_send,
    ring_recv,
    weight_send,
    weight_recv,
    plane_send,
    plane_recv,
    share_send,
    share_recv,
):
    seq_here, tp_here = lax.axis_index("seq"), lax.axis_index("tp")
    z, lane = seq_here // LANES, seq_here % LANES
    row, core = lane // 2, lane % 2
    inside = tp_here * LANES + lane
    crowd = GROUPS * LANES

    def plane_at(step):
        return (z + step + PLANES) % PLANES

    up = (plane_at(1) * LANES + lane, tp_here)
    down = (plane_at(-1) * LANES + lane, tp_here)

    barrier = pltpu.get_barrier_semaphore()

    def greet(device):
        pl.semaphore_signal(barrier, inc=1, device_id=device, device_id_type=MESH)

    greet(up)
    greet(down)

    def greet_inside(step):
        other = (inside + step) % crowd
        greet((z * LANES + other % LANES, other // LANES))

    each(1, crowd, greet_inside)

    def weight_copy(piece, way):
        return pltpu.make_async_remote_copy(
            src_ref=weight_buf.at[piece],
            dst_ref=weight_buf.at[piece],
            send_sem=weight_send.at[way, piece],
            recv_sem=weight_recv.at[piece],
            device_id=up if way == 0 else down,
            device_id_type=MESH,
        )

    def ring_copy(piece, which, way):
        return pltpu.make_async_remote_copy(
            src_ref=kv_buf.at[piece, which],
            dst_ref=kv_buf.at[piece, which],
            send_sem=ring_send.at[way, piece, which],
            recv_sem=ring_recv.at[piece, which],
            device_id=up if way == 0 else down,
            device_id_type=MESH,
        )

    def stage_copy(source, dest):
        return pltpu.make_async_remote_copy(
            src_ref=send_buf.at[dest],
            dst_ref=stage_buf.at[source],
            send_sem=stage_send.at[dest],
            recv_sem=stage_recv.at[source],
            device_id=(z * LANES + dest, tp_here),
            device_id_type=MESH,
        )

    def weight_step(step, last=False):
        weight_copy(plane_at(-step), 0).wait_recv()
        if not last:
            weight_copy(plane_at(-step), 0).start()
        weight_copy(plane_at(step), 1).wait_recv()

    weight_buf[z] = weight_ref[...]

    lanes = lax.broadcasted_iota(jnp.int32, (SPAN, DH), 1)
    frequency = jnp.exp((lanes % 32).astype(jnp.float32) * (-math.log(100.0) / 32))
    place = jnp.where(lanes < DH // 2, position_ref[:, 0:1], position_ref[:, 1:2])
    angle = place.astype(jnp.float32) * frequency
    first = lanes % 64 < 32
    cosine = jnp.cos(angle)
    sine = jnp.sin(angle)
    sine = jnp.where(first, -sine, sine)

    def rotate(states):
        states = states.astype(jnp.float32)
        partner = jnp.where(
            first, pltpu.roll(states, DH - 32, axis=1), pltpu.roll(states, 32, axis=1)
        )
        return (states * cosine + partner * sine).astype(jnp.bfloat16)

    pl.semaphore_wait(barrier, 2 + crowd - 1)
    weight_copy(z, 0).start()
    weight_copy(z, 1).start()

    for head in range(LANES):
        features = slice(head * DH, (head + 1) * DH)
        send_buf[head, 0] = rotate(query_ref[:, features])
        send_buf[head, 1] = rotate(key_ref[:, features])
        send_buf[head, 2] = value_ref[:, features]

        @pl.when(head != lane)
        def _(head=head):
            stage_copy(lane, head).start()

    stage_buf[lane] = send_buf[lane]

    for part in range(TOKENS // CHUNK):
        own = segment_ref[pl.ds(z * (TOKENS // CHUNK) + part, 1), :].astype(jnp.float32)
        query_segment[part * CHUNK:(part + 1) * CHUNK] = jnp.broadcast_to(own, (CHUNK, CHUNK)).T
    peak_ref[...] = jnp.full(peak_ref.shape, masked_score, jnp.float32)
    total_ref[...] = jnp.zeros(total_ref.shape, jnp.float32)
    sum_ref[...] = jnp.zeros(sum_ref.shape, jnp.float32)

    weight_copy(plane_at(-1), 0).wait_recv()
    weight_copy(plane_at(-1), 0).start()
    weight_copy(plane_at(1), 1).wait_recv()
    weight_copy(plane_at(1), 1).start()

    each(1, LANES, lambda step: stage_copy((lane + step) % LANES, lane).wait_recv())
    for which in range(2):
        kv_buf[z, which] = stage_buf[:, 1 + which].reshape(TOKENS, DH)
        for way in range(2):
            ring_copy(z, which, way).start()

    def attend(piece):
        key = kv_buf[piece, 0]
        value = kv_buf[piece, 1]
        parts = TOKENS // CHUNK
        key_segment = [
            segment_ref[pl.ds(piece * parts + part, 1), :].astype(jnp.float32)
            for part in range(parts)
        ]
        for chunk in range(parts):
            rows = slice(chunk * CHUNK, (chunk + 1) * CHUNK)
            per = CHUNK // SPAN
            query = stage_buf[chunk * per:(chunk + 1) * per, 0].reshape(CHUNK, DH)
            score = lax.dot_general(
                query, key, (((1,), (1,)), ((), ())), preferred_element_type=jnp.float32
            )
            segment = query_segment[rows]
            scores = [
                jnp.where(
                    segment == key_segment[part],
                    score[:, part * CHUNK:(part + 1) * CHUNK],
                    masked_score,
                )
                for part in range(parts)
            ]
            top = jnp.maximum(
                jnp.maximum(scores[0], scores[1]), jnp.maximum(scores[2], scores[3])
            )
            old = peak_ref[rows]
            peak = jnp.maximum(old, jnp.max(top, axis=1, keepdims=True))
            peak_ref[rows] = peak
            fade = jnp.exp2((old - peak) * EXPONENT_SCALE)
            exponents = [jnp.exp2((part - peak) * EXPONENT_SCALE) for part in scores]
            total_ref[rows] = total_ref[rows] * fade + (
                (exponents[0] + exponents[1]) + (exponents[2] + exponents[3])
            )
            weights = jnp.concatenate([part.astype(jnp.bfloat16) for part in exponents], axis=1)
            sum_ref[rows] = sum_ref[rows] * fade + jnp.dot(
                weights, value, preferred_element_type=jnp.float32
            )

    def ring_step(step):
        below, above = plane_at(-step), plane_at(step)
        open_still = step < HALF_RING - 1
        ring_copy(below, 0, 0).wait_recv()
        ring_copy(below, 0, 0).start()
        ring_copy(above, 0, 1).wait_recv()

        @pl.when(open_still)
        def _():
            ring_copy(above, 0, 1).start()

        attend(plane_at(step - 1))

        ring_copy(below, 1, 0).wait_recv()

        @pl.when(open_still)
        def _():
            ring_copy(below, 1, 0).start()

        ring_copy(above, 1, 1).wait_recv()
        ring_copy(above, 1, 1).start()

        @pl.when(open_still)
        def _():
            weight_copy(plane_at(-step - 1), 0).wait_recv()
            weight_copy(plane_at(-step - 1), 0).start()
            weight_copy(plane_at(step + 1), 1).wait_recv()

        @pl.when(step < HALF_RING - 2)
        def _():
            weight_copy(plane_at(step + 1), 1).start()

        attend(below)

    each(1, HALF_RING, ring_step)
    attend(plane_at(HALF_RING - 1))
    ring_copy(plane_at(HALF_RING), 0, 0).wait_recv()
    ring_copy(plane_at(HALF_RING), 1, 1).wait_recv()
    attend(plane_at(HALF_RING))

    total = jnp.sum(total_ref[...], axis=1, keepdims=True)
    plane_buf[lane] = (sum_ref[...] / total).astype(jnp.bfloat16)

    def plane_copy(slot, device_lane):
        return pltpu.make_async_remote_copy(
            src_ref=plane_buf.at[slot],
            dst_ref=plane_buf.at[slot],
            send_sem=plane_send.at[slot, device_lane],
            recv_sem=plane_recv.at[slot],
            device_id=(z * LANES + device_lane, tp_here),
            device_id_type=MESH,
        )

    sibling = row * 2 + 1 - core

    def mate(step):
        return ((row + step) % GROUPS) * 2 + core

    def sibling_of(step):
        return ((row + step) % GROUPS) * 2 + 1 - core

    each(1, GROUPS, lambda step: plane_copy(lane, mate(step)).start())
    plane_copy(lane, sibling).start()

    def pass_on(step):
        plane_copy(mate(step), lane).wait_recv()
        plane_copy(mate(step), sibling).start()

    each(1, GROUPS, pass_on)
    each(0, GROUPS, lambda step: plane_copy(sibling_of(step), lane).wait_recv())

    weight_copy(plane_at(HALF_RING), 0).wait_recv()
    weight = weight_buf[...].reshape(PLANES * weight_ref.shape[0], LANES * DH)
    rows = TOKENS // 2
    for half in range(2):
        token = jnp.concatenate(
            [plane_buf[head, half * rows:(half + 1) * rows] for head in range(LANES)], axis=1
        )
        part = lax.dot_general(
            token, weight, (((1,), (1,)), ((), ())), preferred_element_type=jnp.float32
        ).astype(jnp.bfloat16)
        for group in range(GROUPS):
            part_buf[group, half * (LANES // 2):(half + 1) * (LANES // 2)] = part[
                :, group * DH:(group + 1) * DH
            ].reshape(LANES // 2, SPAN, DH)

    def share_copy(source, dest):
        return pltpu.make_async_remote_copy(
            src_ref=part_buf.at[dest // LANES, dest % LANES],
            dst_ref=share_buf.at[source // LANES, source % LANES],
            send_sem=share_send.at[dest],
            recv_sem=share_recv.at[source],
            device_id=(z * LANES + dest % LANES, dest // LANES),
            device_id_type=MESH,
        )

    each(1, crowd, lambda step: share_copy(inside, (inside + step) % crowd).start())
    share_buf[tp_here, lane] = part_buf[tp_here, lane]
    each(1, crowd, lambda step: share_copy((inside + step) % crowd, inside).wait_recv())

    sums = []
    for source in range(LANES):
        add = share_buf[0, source].astype(jnp.float32)
        for group in range(1, GROUPS):
            add = add + share_buf[group, source].astype(jnp.float32)
        sums.append(add)
    for quarter in range(4):
        for half in range(2):
            projected = jnp.concatenate(
                [sums[half * 4 + i][:, quarter * 32:(quarter + 1) * 32] for i in range(4)], axis=1
            )
            columns = slice((quarter * 2 + half) * DH, (quarter * 2 + half + 1) * DH)
            encoded = residual_ref[:, columns].astype(jnp.float32) + gain_ref[:, columns] * projected
            encoded_ref[:, columns] = encoded.astype(encoded_ref.dtype)

    each(1, LANES, lambda step: stage_copy(lane, (lane + step) % LANES).wait_send())

    def ring_sent(step):
        ring_copy(plane_at(-step), 0, 0).wait_send()
        ring_copy(plane_at(step), 1, 1).wait_send()
        weight_copy(plane_at(-step), 0).wait_send()

        @pl.when(step < HALF_RING - 1)
        def _():
            ring_copy(plane_at(-step), 1, 0).wait_send()
            ring_copy(plane_at(step), 0, 1).wait_send()
            weight_copy(plane_at(step), 1).wait_send()

    each(0, HALF_RING, ring_sent)
    each(1, GROUPS, lambda step: plane_copy(lane, mate(step)).wait_send())
    each(0, GROUPS, lambda step: plane_copy(mate(step), sibling).wait_send())
    each(1, crowd, lambda step: share_copy(inside, (inside + step) % crowd).wait_send())


def local(
    query_states,
    key_states,
    value_states,
    residual,
    segment_ids,
    positions,
    out_weight,
    layer_scale,
):
    vmem = pl.BlockSpec(memory_space=pltpu.VMEM)
    columns, features = out_weight.shape[1], out_weight.shape[0]
    dma = pltpu.SemaphoreType.DMA
    return pl.pallas_call(
        layer_kernel,
        out_shape=jax.ShapeDtypeStruct(residual.shape, jnp.bfloat16),
        in_specs=[vmem] * 8,
        out_specs=vmem,
        scratch_shapes=[
            pltpu.VMEM((LANES, 3, SPAN, DH), jnp.bfloat16),
            pltpu.VMEM((LANES, 3, SPAN, DH), jnp.bfloat16),
            pltpu.VMEM((PLANES, 2, TOKENS, DH), jnp.bfloat16),
            pltpu.VMEM((PLANES, columns, features), jnp.bfloat16),
            pltpu.VMEM((TOKENS, CHUNK), jnp.float32),
            pltpu.VMEM((TOKENS, DH), jnp.float32),
            pltpu.VMEM((TOKENS, DH), jnp.float32),
            pltpu.VMEM((TOKENS, DH), jnp.float32),
            pltpu.VMEM((LANES, TOKENS, DH), jnp.bfloat16),
            pltpu.VMEM((GROUPS, LANES, SPAN, DH), jnp.bfloat16),
            pltpu.VMEM((GROUPS, LANES, SPAN, DH), jnp.bfloat16),
            dma((LANES,)),
            dma((LANES,)),
            dma((2, PLANES, 2)),
            dma((PLANES, 2)),
            dma((2, PLANES)),
            dma((PLANES,)),
            dma((LANES, LANES)),
            dma((LANES,)),
            dma((GROUPS * LANES,)),
            dma((GROUPS * LANES,)),
        ],
        compiler_params=pltpu.CompilerParams(
            collective_id=0, has_side_effects=True, vmem_limit_bytes=40 * 1024 * 1024
        ),
    )(
        query_states,
        key_states,
        value_states,
        residual,
        segment_ids.reshape(-1, CHUNK),
        positions.T,
        out_weight.T,
        layer_scale[None, :],
    )


def solution(mesh):
    in_specs = (
        P("seq", "tp"),
        P("seq", "tp"),
        P("seq", "tp"),
        P("seq", "tp"),
        P(),
        P(None, "seq"),
        P("tp", "seq"),
        P("tp"),
    )
    out_specs = P("seq", "tp")
    return jax.shard_map(local, mesh=mesh, in_specs=in_specs, out_specs=out_specs, check_vma=False)
```

```python
import math

import jax
import jax.numpy as jnp
from jax import lax
from jax.experimental import pallas as pl
from jax.experimental.pallas import tpu as pltpu
from jax.sharding import PartitionSpec as P

DH = 128
PLANES = 16
LANES = 8
GROUPS = 4
SPAN = 64
TOKENS = LANES * SPAN
CHUNK = 128
HALF_RING = PLANES // 2
PIECES = 4
PARTS = TOKENS // CHUNK
PER_PART = LANES // PARTS
EXPONENT_SCALE = DH ** (-0.5) * math.log2(math.e)
MESH = pl.DeviceIdType.MESH

masked_score = -1e30


def each(start, stop, act):
    def body(step, carry):
        act(step)
        return carry

    lax.fori_loop(start, stop, body, 0)


def layer_kernel(
    query_ref,
    key_ref,
    value_ref,
    residual_ref,
    segment_ref,
    position_ref,
    weight_ref,
    gain_ref,
    encoded_ref,
    query_buf,
    key_buf,
    value_buf,
    residual_buf,
    send_buf,
    stage_buf,
    kv_buf,
    weight_buf,
    query_segment,
    peak_ref,
    total_ref,
    sum_ref,
    plane_buf,
    part_buf,
    share_buf,
    stage_send,
    stage_recv,
    ring_send,
    ring_recv,
    weight_send,
    weight_recv,
    mate_send,
    sibling_send,
    plane_recv,
    share_send,
    share_recv,
    load_sem,
):
    seq_here, tp_here = lax.axis_index("seq"), lax.axis_index("tp")
    z, lane = seq_here // LANES, seq_here % LANES
    row, core = lane // 2, lane % 2
    inside = tp_here * LANES + lane
    crowd = GROUPS * LANES

    def plane_at(step):
        return (z + step + PLANES) % PLANES

    loads = [
        pltpu.make_async_copy(source, dest, load_sem.at[index])
        for index, (source, dest) in enumerate(
            [
                (query_ref, query_buf),
                (key_ref, key_buf),
                (value_ref, value_buf),
                (weight_ref, weight_buf.at[z]),
                (residual_ref, residual_buf),
            ]
        )
    ]
    for load in loads:
        load.start()

    up = (plane_at(1) * LANES + lane, tp_here)
    down = (plane_at(-1) * LANES + lane, tp_here)

    barrier = pltpu.get_barrier_semaphore()

    def greet(device):
        pl.semaphore_signal(barrier, inc=1, device_id=device, device_id_type=MESH)

    greet(up)
    greet(down)

    def greet_inside(step):
        other = (inside + step) % crowd
        greet((z * LANES + other % LANES, other // LANES))

    each(1, crowd, greet_inside)

    def weight_copy(plane, way):
        return pltpu.make_async_remote_copy(
            src_ref=weight_buf.at[plane],
            dst_ref=weight_buf.at[plane],
            send_sem=weight_send.at[way, plane],
            recv_sem=weight_recv.at[plane],
            device_id=up if way == 0 else down,
            device_id_type=MESH,
        )

    def ring_copy(plane, piece, way):
        return pltpu.make_async_remote_copy(
            src_ref=kv_buf.at[plane, piece],
            dst_ref=kv_buf.at[plane, piece],
            send_sem=ring_send.at[way, plane, piece],
            recv_sem=ring_recv.at[plane, piece],
            device_id=up if way == 0 else down,
            device_id_type=MESH,
        )

    def stage_copy(source, dest):
        return pltpu.make_async_remote_copy(
            src_ref=send_buf.at[dest],
            dst_ref=stage_buf.at[source],
            send_sem=stage_send.at[dest],
            recv_sem=stage_recv.at[source],
            device_id=(z * LANES + dest, tp_here),
            device_id_type=MESH,
        )

    def weight_hop(hop):
        weight_copy(plane_at(-hop), 0).wait_recv()
        weight_copy(plane_at(-hop), 0).start()
        weight_copy(plane_at(hop), 1).wait_recv()
        weight_copy(plane_at(hop), 1).start()

    lanes = lax.broadcasted_iota(jnp.int32, (SPAN, DH), 1)
    frequency = jnp.exp((lanes % 32).astype(jnp.float32) * (-math.log(100.0) / 32))
    grid_row, grid_column = [
        jnp.broadcast_to(position_ref[axis:axis + 1, :].astype(jnp.float32), (DH, SPAN)).T
        for axis in range(2)
    ]
    angle = jnp.where(lanes < DH // 2, grid_row, grid_column) * frequency
    first = lanes % 64 < 32
    cosine = jnp.cos(angle)
    sine = jnp.sin(angle)
    sine = jnp.where(first, -sine, sine)

    def rotate(states):
        states = states.astype(jnp.float32)
        partner = jnp.where(
            first, pltpu.roll(states, DH - 32, axis=1), pltpu.roll(states, 32, axis=1)
        )
        return (states * cosine + partner * sine).astype(jnp.bfloat16)

    for load in loads[:3]:
        load.wait()
    for head in range(LANES):
        features = slice(head * DH, (head + 1) * DH)
        send_buf[head, 0] = rotate(query_buf[:, features])
        send_buf[head, 1] = rotate(key_buf[:, features])
        send_buf[head, 2] = value_buf[:, features]
    loads[3].wait()

    pl.semaphore_wait(barrier, 2 + crowd - 1)
    weight_copy(z, 0).start()
    weight_copy(z, 1).start()
    each(1, LANES, lambda step: stage_copy(lane, (lane + step) % LANES).start())
    stage_buf[lane] = send_buf[lane]

    for part in range(PARTS):
        own = segment_ref[pl.ds(z * PARTS + part, 1), :].astype(jnp.float32)
        query_segment[part * CHUNK:(part + 1) * CHUNK] = jnp.broadcast_to(own, (CHUNK, CHUNK)).T
    peak_ref[...] = jnp.full(peak_ref.shape, masked_score, jnp.float32)
    total_ref[...] = jnp.zeros(total_ref.shape, jnp.float32)
    sum_ref[...] = jnp.zeros(sum_ref.shape, jnp.float32)

    def attend(plane, chunk):
        key = kv_buf[plane, 0:2].reshape(TOKENS, DH)
        value = kv_buf[plane, 2:4].reshape(TOKENS, DH)
        rows = slice(chunk * CHUNK, (chunk + 1) * CHUNK)
        query = stage_buf[chunk * PER_PART:(chunk + 1) * PER_PART, 0].reshape(CHUNK, DH)
        score = lax.dot_general(
            query, key, (((1,), (1,)), ((), ())), preferred_element_type=jnp.float32
        )
        segment = query_segment[rows]
        scores = [
            jnp.where(
                segment == segment_ref[pl.ds(plane * PARTS + part, 1), :].astype(jnp.float32),
                score[:, part * CHUNK:(part + 1) * CHUNK],
                masked_score,
            )
            for part in range(PARTS)
        ]
        top = jnp.maximum(
            jnp.maximum(scores[0], scores[1]), jnp.maximum(scores[2], scores[3])
        )
        old = peak_ref[rows]
        peak = jnp.maximum(old, jnp.max(top, axis=1, keepdims=True))
        peak_ref[rows] = peak
        fade = jnp.exp2((old - peak) * EXPONENT_SCALE)
        exponents = [jnp.exp2((part - peak) * EXPONENT_SCALE) for part in scores]
        total_ref[rows] = total_ref[rows] * fade + (
            (exponents[0] + exponents[1]) + (exponents[2] + exponents[3])
        )
        weights = jnp.concatenate([part.astype(jnp.bfloat16) for part in exponents], axis=1)
        sum_ref[rows] = sum_ref[rows] * fade + jnp.dot(
            weights, value, preferred_element_type=jnp.float32
        )

    weight_hop(1)
    weight_hop(2)

    each(1, LANES, lambda step: stage_copy((lane + step) % LANES, lane).wait_recv())
    for which in range(2):
        states = stage_buf[:, 1 + which].reshape(2, TOKENS // 2, DH)
        kv_buf[z, 2 * which:2 * which + 2] = states
    for piece in range(PIECES):
        ring_copy(z, piece, 0).start()
        ring_copy(z, piece, 1).start()
        attend(z, piece)

    def ring_step(step):
        below, above = plane_at(-step), plane_at(step)
        for piece in range(PIECES):
            keys = piece < PIECES // 2
            ring_copy(below, piece, 0).wait_recv()
            if keys:
                ring_copy(below, piece, 0).start()
            else:
                pl.when(step < HALF_RING - 1)(lambda: ring_copy(below, piece, 0).start())
            ring_copy(above, piece, 1).wait_recv()
            if keys:
                pl.when(step < HALF_RING - 1)(lambda: ring_copy(above, piece, 1).start())
            else:
                ring_copy(above, piece, 1).start()

            @pl.when(step > 1)
            def _():
                attend(plane_at(1 - step), piece)
                attend(plane_at(step - 1), piece)

        @pl.when(jnp.logical_and(step % 2 == 1, step < HALF_RING - 1))
        def _():
            weight_hop(3 + step // 2)

    each(1, HALF_RING, ring_step)
    far = plane_at(HALF_RING)
    for piece in range(PIECES):
        ring_copy(far, piece, 0 if piece < PIECES // 2 else 1).wait_recv()
        attend(plane_at(1 - HALF_RING), piece)
        attend(plane_at(HALF_RING - 1), piece)
    weight_hop(6)

    sibling = row * 2 + 1 - core

    def mate(step):
        return ((row + step) % GROUPS) * 2 + core

    def sibling_of(step):
        return ((row + step) % GROUPS) * 2 + 1 - core

    def plane_copy(slot, chunk, device_lane, send_sem):
        return pltpu.make_async_remote_copy(
            src_ref=plane_buf.at[slot, chunk],
            dst_ref=plane_buf.at[slot, chunk],
            send_sem=send_sem,
            recv_sem=plane_recv.at[slot, chunk],
            device_id=(z * LANES + device_lane, tp_here),
            device_id_type=MESH,
        )

    def to_mate(step, chunk):
        return plane_copy(lane, chunk, mate(step), mate_send.at[step, chunk])

    def to_sibling(step, chunk):
        return plane_copy(mate(step), chunk, sibling, sibling_send.at[step, chunk])

    def from_sibling(step, chunk):
        return plane_copy(sibling_of(step), chunk, lane, sibling_send.at[step, chunk])

    for chunk in range(PARTS):
        attend(far, chunk)
        rows = slice(chunk * CHUNK, (chunk + 1) * CHUNK)
        total = jnp.sum(total_ref[rows], axis=1, keepdims=True)
        plane_buf[lane, chunk] = (sum_ref[rows] / total).astype(jnp.bfloat16)
        each(1, GROUPS, lambda step: to_mate(step, chunk).start())
        to_sibling(0, chunk).start()

    weight_copy(plane_at(-7), 0).wait_recv()
    weight_copy(plane_at(-7), 0).start()
    weight_copy(plane_at(7), 1).wait_recv()

    def pass_on(chunk):
        def act(step):
            to_sibling(step, chunk).wait_recv()
            to_sibling(step, chunk).start()

        each(1, GROUPS, act)

    def share_copy(source, dest):
        return pltpu.make_async_remote_copy(
            src_ref=part_buf.at[dest // LANES, dest % LANES],
            dst_ref=share_buf.at[source // LANES, source % LANES],
            send_sem=share_send.at[dest],
            recv_sem=share_recv.at[source],
            device_id=(z * LANES + dest % LANES, dest // LANES),
            device_id_type=MESH,
        )

    pass_on(0)
    for chunk in range(PARTS):
        if chunk + 1 < PARTS:
            pass_on(chunk + 1)
        if chunk == 0:
            weight_copy(far, 0).wait_recv()
        each(0, GROUPS, lambda step: from_sibling(step, chunk).wait_recv())
        token = jnp.concatenate([plane_buf[head, chunk] for head in range(LANES)], axis=1)
        part = lax.dot_general(
            token,
            weight_buf[...].reshape(GROUPS * DH, LANES * DH),
            (((1,), (1,)), ((), ())),
            preferred_element_type=jnp.float32,
        ).astype(jnp.bfloat16)
        for group in range(GROUPS):
            part_buf[group, chunk * PER_PART:(chunk + 1) * PER_PART] = part[
                :, group * DH:(group + 1) * DH
            ].reshape(PER_PART, SPAN, DH)

        def share_out(step):
            dest = ((tp_here + step // PER_PART) % GROUPS) * LANES + chunk * PER_PART + step % PER_PART
            pl.when(dest != inside)(lambda: share_copy(inside, dest).start())

        each(0, GROUPS * PER_PART, share_out)

    share_buf[tp_here, lane] = part_buf[tp_here, lane]
    loads[4].wait()
    each(1, crowd, lambda step: share_copy((inside + step) % crowd, inside).wait_recv())

    sums = []
    for source in range(LANES):
        add = share_buf[0, source].astype(jnp.float32)
        for group in range(1, GROUPS):
            add = add + share_buf[group, source].astype(jnp.float32)
        sums.append(add)
    for quarter in range(4):
        for half in range(2):
            projected = jnp.concatenate(
                [sums[half * 4 + i][:, quarter * 32:(quarter + 1) * 32] for i in range(4)], axis=1
            )
            columns = slice((quarter * 2 + half) * DH, (quarter * 2 + half + 1) * DH)
            encoded = residual_buf[:, columns].astype(jnp.float32) + gain_ref[:, columns] * projected
            encoded_ref[:, columns] = encoded.astype(encoded_ref.dtype)

    each(1, LANES, lambda step: stage_copy(lane, (lane + step) % LANES).wait_send())

    def ring_sent(step):
        for piece in range(PIECES // 2):
            ring_copy(plane_at(-step), piece, 0).wait_send()
            ring_copy(plane_at(step), PIECES // 2 + piece, 1).wait_send()
        weight_copy(plane_at(-step), 0).wait_send()

        @pl.when(step < HALF_RING - 1)
        def _():
            for piece in range(PIECES // 2):
                ring_copy(plane_at(-step), PIECES // 2 + piece, 0).wait_send()
                ring_copy(plane_at(step), piece, 1).wait_send()
            weight_copy(plane_at(step), 1).wait_send()

    each(0, HALF_RING, ring_sent)

    def plane_sent(chunk):
        each(1, GROUPS, lambda step: to_mate(step, chunk).wait_send())
        each(0, GROUPS, lambda step: to_sibling(step, chunk).wait_send())

    each(0, PARTS, plane_sent)
    each(1, crowd, lambda step: share_copy(inside, (inside + step) % crowd).wait_send())


def local(
    query_states,
    key_states,
    value_states,
    residual,
    segment_ids,
    positions,
    out_weight,
    layer_scale,
):
    vmem = pl.BlockSpec(memory_space=pltpu.VMEM)
    hbm = pl.BlockSpec(memory_space=pltpu.HBM)
    columns, features = out_weight.shape[1], out_weight.shape[0]
    dma = pltpu.SemaphoreType.DMA
    return pl.pallas_call(
        layer_kernel,
        out_shape=jax.ShapeDtypeStruct(residual.shape, jnp.bfloat16),
        in_specs=[hbm, hbm, hbm, hbm, vmem, vmem, hbm, vmem],
        out_specs=vmem,
        scratch_shapes=[
            pltpu.VMEM(query_states.shape, jnp.bfloat16),
            pltpu.VMEM(query_states.shape, jnp.bfloat16),
            pltpu.VMEM(query_states.shape, jnp.bfloat16),
            pltpu.VMEM(query_states.shape, jnp.bfloat16),
            pltpu.VMEM((LANES, 3, SPAN, DH), jnp.bfloat16),
            pltpu.VMEM((LANES, 3, SPAN, DH), jnp.bfloat16),
            pltpu.VMEM((PLANES, PIECES, TOKENS // 2, DH), jnp.bfloat16),
            pltpu.VMEM((PLANES, columns, features), jnp.bfloat16),
            pltpu.VMEM((TOKENS, CHUNK), jnp.float32),
            pltpu.VMEM((TOKENS, DH), jnp.float32),
            pltpu.VMEM((TOKENS, DH), jnp.float32),
            pltpu.VMEM((TOKENS, DH), jnp.float32),
            pltpu.VMEM((LANES, PARTS, CHUNK, DH), jnp.bfloat16),
            pltpu.VMEM((GROUPS, LANES, SPAN, DH), jnp.bfloat16),
            pltpu.VMEM((GROUPS, LANES, SPAN, DH), jnp.bfloat16),
            dma((LANES,)),
            dma((LANES,)),
            dma((2, PLANES, PIECES)),
            dma((PLANES, PIECES)),
            dma((2, PLANES)),
            dma((PLANES,)),
            dma((GROUPS, PARTS)),
            dma((GROUPS, PARTS)),
            dma((LANES, PARTS)),
            dma((GROUPS * LANES,)),
            dma((GROUPS * LANES,)),
            dma((5,)),
        ],
        compiler_params=pltpu.CompilerParams(
            collective_id=0, has_side_effects=True, vmem_limit_bytes=56 * 1024 * 1024
        ),
    )(
        query_states,
        key_states,
        value_states,
        residual,
        segment_ids.reshape(-1, CHUNK),
        positions,
        out_weight.T,
        layer_scale[None, :],
    )


def solution(mesh):
    in_specs = (
        P("seq", "tp"),
        P("seq", "tp"),
        P("seq", "tp"),
        P("seq", "tp"),
        P(),
        P(None, "seq"),
        P("tp", "seq"),
        P("tp"),
    )
    out_specs = P("seq", "tp")
    return jax.shard_map(local, mesh=mesh, in_specs=in_specs, out_specs=out_specs, check_vma=False)
```

```python
import math

import jax
import jax.numpy as jnp
from jax import lax
from jax.experimental import pallas as pl
from jax.experimental.pallas import tpu as pltpu
from jax.sharding import PartitionSpec as P

DH = 128
PLANES = 16
LANES = 8
GROUPS = 4
SPAN = 64
TOKENS = LANES * SPAN
CHUNK = 128
HALF_RING = PLANES // 2
PIECES = 4
KEYS = PIECES // 2
SOURCES = LANES // KEYS
PARTS = TOKENS // CHUNK
PER_PART = LANES // PARTS
TAIL = 4
TAIL_ROWS = TOKENS // TAIL
PER_TAIL = LANES // TAIL
EXPONENT_SCALE = DH ** (-0.5) * math.log2(math.e)
MESH = pl.DeviceIdType.MESH

masked_score = -1e30


def each(start, stop, act):
    def body(step, carry):
        act(step)
        return carry

    lax.fori_loop(start, stop, body, 0)


def layer_kernel(
    query_ref,
    key_ref,
    value_ref,
    residual_ref,
    segment_ref,
    position_ref,
    weight_ref,
    gain_ref,
    encoded_ref,
    query_buf,
    key_buf,
    value_buf,
    residual_buf,
    send_buf,
    stage_buf,
    kv_buf,
    weight_buf,
    query_segment,
    peak_ref,
    total_ref,
    sum_ref,
    plane_buf,
    part_buf,
    share_buf,
    stage_send,
    stage_recv,
    ring_send,
    ring_recv,
    weight_send,
    weight_recv,
    plane_send,
    plane_recv,
    share_send,
    share_recv,
    load_sem,
):
    seq_here, tp_here = lax.axis_index("seq"), lax.axis_index("tp")
    z, lane = seq_here // LANES, seq_here % LANES
    row, core = lane // 2, lane % 2
    inside = tp_here * LANES + lane
    crowd = GROUPS * LANES

    def plane_at(step):
        return (z + step + PLANES) % PLANES

    loads = [
        pltpu.make_async_copy(source, dest, load_sem.at[index])
        for index, (source, dest) in enumerate(
            [
                (query_ref, query_buf),
                (key_ref, key_buf),
                (value_ref, value_buf),
                (weight_ref, weight_buf.at[z]),
                (residual_ref, residual_buf),
            ]
        )
    ]
    for load in loads:
        load.start()

    up = (plane_at(1) * LANES + lane, tp_here)
    down = (plane_at(-1) * LANES + lane, tp_here)

    barrier = pltpu.get_barrier_semaphore()

    def greet(device):
        pl.semaphore_signal(barrier, inc=1, device_id=device, device_id_type=MESH)

    greet(up)
    greet(down)

    def greet_inside(step):
        other = (inside + step) % crowd
        greet((z * LANES + other % LANES, other // LANES))

    each(1, crowd, greet_inside)

    def weight_copy(plane, way):
        return pltpu.make_async_remote_copy(
            src_ref=weight_buf.at[plane],
            dst_ref=weight_buf.at[plane],
            send_sem=weight_send,
            recv_sem=weight_recv.at[plane],
            device_id=up if way == 0 else down,
            device_id_type=MESH,
        )

    def ring_copy(plane, piece, way):
        return pltpu.make_async_remote_copy(
            src_ref=kv_buf.at[plane, piece],
            dst_ref=kv_buf.at[plane, piece],
            send_sem=ring_send,
            recv_sem=ring_recv.at[plane, piece],
            device_id=up if way == 0 else down,
            device_id_type=MESH,
        )

    def landing(source, which):
        if which == 0:
            return stage_buf.at[source]
        piece = (which - 1) * KEYS + source // SOURCES
        start = pl.multiple_of(source % SOURCES * SPAN, SPAN)
        return kv_buf.at[z, piece, pl.ds(start, SPAN)]

    def stage_copy(source, dest, which):
        return pltpu.make_async_remote_copy(
            src_ref=send_buf.at[which * LANES + dest],
            dst_ref=landing(source, which),
            send_sem=stage_send,
            recv_sem=stage_recv.at[which, source],
            device_id=(z * LANES + dest, tp_here),
            device_id_type=MESH,
        )

    def spread(which):
        each(1, LANES, lambda step: stage_copy(lane, (lane + step) % LANES, which).start())
        landing(lane, which)[...] = send_buf[which * LANES + lane]

    def arrive(which):
        each(1, LANES, lambda step: stage_copy((lane + step) % LANES, lane, which).wait_recv())

    def weight_hop(hop):
        weight_copy(plane_at(-hop), 0).wait_recv()
        weight_copy(plane_at(-hop), 0).start()
        weight_copy(plane_at(hop), 1).wait_recv()
        weight_copy(plane_at(hop), 1).start()

    lanes = lax.broadcasted_iota(jnp.int32, (SPAN, DH), 1)
    frequency = jnp.exp((lanes % 32).astype(jnp.float32) * (-math.log(100.0) / 32))
    grid_row, grid_column = [
        jnp.broadcast_to(position_ref[axis:axis + 1, :].astype(jnp.float32), (DH, SPAN)).T
        for axis in range(2)
    ]
    angle = jnp.where(lanes < DH // 2, grid_row, grid_column) * frequency
    first = lanes % 64 < 32
    cosine = jnp.cos(angle)
    sine = jnp.sin(angle)
    sine = jnp.where(first, -sine, sine)

    def rotate(states):
        states = states.astype(jnp.float32)
        partner = jnp.where(
            first, pltpu.roll(states, DH - 32, axis=1), pltpu.roll(states, 32, axis=1)
        )
        return (states * cosine + partner * sine).astype(jnp.bfloat16)

    loads[1].wait()
    for head in range(LANES):
        send_buf[LANES + head] = rotate(key_buf[:, head * DH:(head + 1) * DH])
    loads[3].wait()

    pl.semaphore_wait(barrier, 2 + crowd - 1)
    spread(1)
    weight_copy(z, 0).start()
    weight_copy(z, 1).start()
    loads[2].wait()
    for head in range(LANES):
        send_buf[2 * LANES + head] = value_buf[:, head * DH:(head + 1) * DH]
    spread(2)
    loads[0].wait()
    for head in range(LANES):
        send_buf[head] = rotate(query_buf[:, head * DH:(head + 1) * DH])
    spread(0)

    for part in range(PARTS):
        own = segment_ref[pl.ds(z * PARTS + part, 1), :].astype(jnp.float32)
        query_segment[part * CHUNK:(part + 1) * CHUNK] = jnp.broadcast_to(own, (CHUNK, CHUNK)).T
    peak_ref[...] = jnp.full(peak_ref.shape, masked_score, jnp.float32)
    total_ref[...] = jnp.zeros(total_ref.shape, jnp.float32)
    sum_ref[...] = jnp.zeros(sum_ref.shape, jnp.float32)

    def attend(plane, chunk):
        key = kv_buf[plane, :KEYS].reshape(TOKENS, DH)
        value = kv_buf[plane, KEYS:].reshape(TOKENS, DH)
        rows = slice(chunk * CHUNK, (chunk + 1) * CHUNK)
        query = stage_buf[chunk * PER_PART:(chunk + 1) * PER_PART].reshape(CHUNK, DH)
        score = lax.dot_general(
            query, key, (((1,), (1,)), ((), ())), preferred_element_type=jnp.float32
        )
        segment = query_segment[rows]
        scores = [
            jnp.where(
                segment == segment_ref[pl.ds(plane * PARTS + part, 1), :].astype(jnp.float32),
                score[:, part * CHUNK:(part + 1) * CHUNK],
                masked_score,
            )
            for part in range(PARTS)
        ]
        top = jnp.maximum(
            jnp.maximum(scores[0], scores[1]), jnp.maximum(scores[2], scores[3])
        )
        old = peak_ref[rows]
        peak = jnp.maximum(old, jnp.max(top, axis=1, keepdims=True))
        peak_ref[rows] = peak
        fade = jnp.exp2((old - peak) * EXPONENT_SCALE)
        exponents = [jnp.exp2((part - peak) * EXPONENT_SCALE) for part in scores]
        total_ref[rows] = total_ref[rows] * fade + (
            (exponents[0] + exponents[1]) + (exponents[2] + exponents[3])
        )
        weights = jnp.concatenate([part.astype(jnp.bfloat16) for part in exponents], axis=1)
        sum_ref[rows] = sum_ref[rows] * fade + jnp.dot(
            weights, value, preferred_element_type=jnp.float32
        )

    for which in range(1, 3):
        arrive(which)
        for piece in range((which - 1) * KEYS, which * KEYS):
            ring_copy(z, piece, 0).start()
            ring_copy(z, piece, 1).start()
        weight_hop(which)
    arrive(0)
    for chunk in range(PARTS):
        attend(z, chunk)

    def quarter(step, index):
        attend(plane_at(-step if index < PARTS else step), index % PARTS)

    def quarters(step, piece):
        for index in range(piece * 2 * PARTS // PIECES, (piece + 1) * 2 * PARTS // PIECES):
            quarter(step, index)

    def ring_step(step):
        below, above = plane_at(-step), plane_at(step)
        for piece in range(PIECES):
            ring_copy(below, piece, 0).wait_recv()
            if piece < KEYS:
                ring_copy(below, piece, 0).start()
            else:
                pl.when(step < HALF_RING - 1)(lambda: ring_copy(below, piece, 0).start())
            ring_copy(above, piece, 1).wait_recv()
            if piece < KEYS:
                pl.when(step < HALF_RING - 1)(lambda: ring_copy(above, piece, 1).start())
            else:
                ring_copy(above, piece, 1).start()
            pl.when(step > 1)(lambda: quarters(step - 1, piece))
        pl.when(step % 2 == 1)(lambda: weight_hop(3 + step // 2))

    each(1, HALF_RING, ring_step)
    far = plane_at(HALF_RING)
    for piece in range(PIECES):
        ring_copy(far, piece, 0 if piece < KEYS else 1).wait_recv()
        quarters(HALF_RING - 1, piece)
    weight_copy(plane_at(-7), 0).wait_recv()
    weight_copy(plane_at(-7), 0).start()
    weight_copy(plane_at(7), 1).wait_recv()

    sibling = row * 2 + 1 - core

    def mate(step):
        return ((row + step) % GROUPS) * 2 + core

    def sibling_of(step):
        return ((row + step) % GROUPS) * 2 + 1 - core

    def plane_copy(slot, chunk, device_lane):
        return pltpu.make_async_remote_copy(
            src_ref=plane_buf.at[slot * TAIL + chunk],
            dst_ref=plane_buf.at[slot * TAIL + chunk],
            send_sem=plane_send,
            recv_sem=plane_recv.at[slot, chunk],
            device_id=(z * LANES + device_lane, tp_here),
            device_id_type=MESH,
        )

    def to_mate(step, chunk):
        return plane_copy(lane, chunk, mate(step))

    def to_sibling(step, chunk):
        return plane_copy(mate(step), chunk, sibling)

    def from_sibling(step, chunk):
        return plane_copy(sibling_of(step), chunk, lane)

    for chunk in range(TAIL):
        for quarter_index in range(chunk * PARTS // TAIL, (chunk + 1) * PARTS // TAIL):
            attend(far, quarter_index)
        rows = slice(chunk * TAIL_ROWS, (chunk + 1) * TAIL_ROWS)
        total = jnp.sum(total_ref[rows], axis=1, keepdims=True)
        plane_buf[lane * TAIL + chunk] = (sum_ref[rows] / total).astype(jnp.bfloat16)
        each(1, GROUPS, lambda step: to_mate(step, chunk).start())
        to_sibling(0, chunk).start()

    def pass_on(chunk):
        def act(step):
            to_sibling(step, chunk).wait_recv()
            to_sibling(step, chunk).start()

        each(1, GROUPS, act)

    def share_copy(source, dest):
        return pltpu.make_async_remote_copy(
            src_ref=part_buf.at[dest],
            dst_ref=share_buf.at[source],
            send_sem=share_send,
            recv_sem=share_recv,
            device_id=(z * LANES + dest % LANES, dest // LANES),
            device_id_type=MESH,
        )

    pass_on(0)
    for chunk in range(TAIL):
        if chunk + 1 < TAIL:
            pass_on(chunk + 1)
        if chunk == 0:
            weight_copy(far, 0).wait_recv()
        each(0, GROUPS, lambda step: from_sibling(step, chunk).wait_recv())
        token = jnp.concatenate([plane_buf[head * TAIL + chunk] for head in range(LANES)], axis=1)
        part = lax.dot_general(
            token,
            weight_buf[...].reshape(GROUPS * DH, LANES * DH),
            (((1,), (1,)), ((), ())),
            preferred_element_type=jnp.float32,
        ).astype(jnp.bfloat16)
        for group in range(GROUPS):
            start = group * LANES + chunk * PER_TAIL
            part_buf[start:start + PER_TAIL] = part[
                :, group * DH:(group + 1) * DH
            ].reshape(PER_TAIL, SPAN, DH)

        def share_out(step):
            dest = ((tp_here + step // PER_TAIL) % GROUPS) * LANES + chunk * PER_TAIL + step % PER_TAIL
            pl.when(dest != inside)(lambda: share_copy(inside, dest).start())

        each(0, GROUPS * PER_TAIL, share_out)

    own_share = pltpu.make_async_copy(part_buf.at[inside], share_buf.at[inside], share_recv)
    own_share.start()

    def drain(ref, sem):
        pltpu.make_async_copy(ref, ref, sem).wait()

    drain(send_buf.at[0:3 * (LANES - 1)], stage_send)
    drain(kv_buf.at[0:PLANES - 1], ring_send)
    drain(weight_buf.at[0:PLANES - 1], weight_send)
    drain(plane_buf.at[0:TAIL * (LANES - 1)], plane_send)
    loads[4].wait()
    drain(share_buf, share_recv)

    sums = []
    for source in range(LANES):
        add = share_buf[source].astype(jnp.float32)
        for group in range(1, GROUPS):
            add = add + share_buf[group * LANES + source].astype(jnp.float32)
        sums.append(add)
    for quarter in range(4):
        for half in range(2):
            projected = jnp.concatenate(
                [sums[half * 4 + i][:, quarter * 32:(quarter + 1) * 32] for i in range(4)], axis=1
            )
            columns = slice((quarter * 2 + half) * DH, (quarter * 2 + half + 1) * DH)
            encoded = residual_buf[:, columns].astype(jnp.float32) + gain_ref[:, columns] * projected
            encoded_ref[:, columns] = encoded.astype(encoded_ref.dtype)

    drain(part_buf.at[0:crowd - 1], share_send)


def local(
    query_states,
    key_states,
    value_states,
    residual,
    segment_ids,
    positions,
    out_weight,
    layer_scale,
):
    vmem = pl.BlockSpec(memory_space=pltpu.VMEM)
    hbm = pl.BlockSpec(memory_space=pltpu.HBM)
    columns, features = out_weight.shape[1], out_weight.shape[0]
    dma = pltpu.SemaphoreType.DMA
    return pl.pallas_call(
        layer_kernel,
        out_shape=jax.ShapeDtypeStruct(residual.shape, jnp.bfloat16),
        in_specs=[hbm, hbm, hbm, hbm, vmem, vmem, hbm, vmem],
        out_specs=vmem,
        scratch_shapes=[
            pltpu.VMEM(query_states.shape, jnp.bfloat16),
            pltpu.VMEM(query_states.shape, jnp.bfloat16),
            pltpu.VMEM(query_states.shape, jnp.bfloat16),
            pltpu.VMEM(query_states.shape, jnp.bfloat16),
            pltpu.VMEM((3 * LANES, SPAN, DH), jnp.bfloat16),
            pltpu.VMEM((LANES, SPAN, DH), jnp.bfloat16),
            pltpu.VMEM((PLANES, PIECES, TOKENS // KEYS, DH), jnp.bfloat16),
            pltpu.VMEM((PLANES, columns, features), jnp.bfloat16),
            pltpu.VMEM((TOKENS, CHUNK), jnp.float32),
            pltpu.VMEM((TOKENS, DH), jnp.float32),
            pltpu.VMEM((TOKENS, DH), jnp.float32),
            pltpu.VMEM((TOKENS, DH), jnp.float32),
            pltpu.VMEM((LANES * TAIL, TAIL_ROWS, DH), jnp.bfloat16),
            pltpu.VMEM((GROUPS * LANES, SPAN, DH), jnp.bfloat16),
            pltpu.VMEM((GROUPS * LANES, SPAN, DH), jnp.bfloat16),
            dma(()),
            dma((3, LANES)),
            dma(()),
            dma((PLANES, PIECES)),
            dma(()),
            dma((PLANES,)),
            dma(()),
            dma((LANES, TAIL)),
            dma(()),
            dma(()),
            dma((5,)),
        ],
        compiler_params=pltpu.CompilerParams(
            collective_id=0, has_side_effects=True, vmem_limit_bytes=56 * 1024 * 1024
        ),
    )(
        query_states,
        key_states,
        value_states,
        residual,
        segment_ids.reshape(-1, CHUNK),
        positions,
        out_weight.T,
        layer_scale[None, :],
    )


def solution(mesh):
    in_specs = (
        P("seq", "tp"),
        P("seq", "tp"),
        P("seq", "tp"),
        P("seq", "tp"),
        P(),
        P(None, "seq"),
        P("tp", "seq"),
        P("tp"),
    )
    out_specs = P("seq", "tp")
    return jax.shard_map(local, mesh=mesh, in_specs=in_specs, out_specs=out_specs, check_vma=False)
```

```python
import math

import jax
import jax.numpy as jnp
from jax import lax
from jax.experimental import pallas as pl
from jax.experimental.pallas import tpu as pltpu
from jax.sharding import PartitionSpec as P

DH = 128
PLANES = 16
LANES = 8
GROUPS = 4
SPAN = 64
TOKENS = LANES * SPAN
CHUNK = 128
HALF_RING = PLANES // 2
PIECES = 4
KEYS = PIECES // 2
SOURCES = LANES // KEYS
PARTS = TOKENS // CHUNK
PER_PART = LANES // PARTS
TAIL = 4
TAIL_ROWS = TOKENS // TAIL
PER_TAIL = LANES // TAIL
EXPONENT_SCALE = DH ** (-0.5) * math.log2(math.e)
MESH = pl.DeviceIdType.MESH

masked_score = -1e30


def each(start, stop, act):
    def body(step, carry):
        act(step)
        return carry

    lax.fori_loop(start, stop, body, 0)


def layer_kernel(
    query_ref,
    key_ref,
    value_ref,
    residual_ref,
    segment_ref,
    position_ref,
    weight_ref,
    gain_ref,
    encoded_ref,
    query_buf,
    key_buf,
    value_buf,
    residual_buf,
    send_buf,
    stage_buf,
    kv_buf,
    weight_buf,
    query_segment,
    peak_ref,
    total_ref,
    sum_ref,
    plane_buf,
    part_buf,
    share_buf,
    stage_send,
    stage_recv,
    ring_send,
    ring_recv,
    weight_send,
    weight_recv,
    plane_send,
    plane_recv,
    share_send,
    share_recv,
    load_sem,
):
    seq_here, tp_here = lax.axis_index("seq"), lax.axis_index("tp")
    z, lane = seq_here // LANES, seq_here % LANES
    row, core = lane // 2, lane % 2
    inside = tp_here * LANES + lane
    crowd = GROUPS * LANES

    def plane_at(step):
        return (z + step + PLANES) % PLANES

    loads = [
        pltpu.make_async_copy(source, dest, load_sem.at[index])
        for index, (source, dest) in enumerate(
            [
                (query_ref, query_buf),
                (key_ref, key_buf),
                (value_ref, value_buf),
                (weight_ref, weight_buf.at[z]),
                (residual_ref, residual_buf),
            ]
        )
    ]
    for load in loads:
        load.start()

    up = (plane_at(1) * LANES + lane, tp_here)
    down = (plane_at(-1) * LANES + lane, tp_here)

    barrier = pltpu.get_barrier_semaphore()

    def greet(device):
        pl.semaphore_signal(barrier, inc=1, device_id=device, device_id_type=MESH)

    greet(up)
    greet(down)

    def greet_inside(step):
        other = (inside + step) % crowd
        greet((z * LANES + other % LANES, other // LANES))

    each(1, crowd, greet_inside)

    def weight_copy(plane, way):
        return pltpu.make_async_remote_copy(
            src_ref=weight_buf.at[plane],
            dst_ref=weight_buf.at[plane],
            send_sem=weight_send,
            recv_sem=weight_recv.at[plane],
            device_id=up if way == 0 else down,
            device_id_type=MESH,
        )

    def ring_copy(plane, piece, way):
        return pltpu.make_async_remote_copy(
            src_ref=kv_buf.at[plane, piece],
            dst_ref=kv_buf.at[plane, piece],
            send_sem=ring_send,
            recv_sem=ring_recv.at[plane, piece],
            device_id=up if way == 0 else down,
            device_id_type=MESH,
        )

    def landing(source, which):
        if which == 0:
            return stage_buf.at[source]
        piece = (which - 1) * KEYS + source // SOURCES
        start = pl.multiple_of(source % SOURCES * SPAN, SPAN)
        return kv_buf.at[z, piece, pl.ds(start, SPAN)]

    def stage_copy(source, dest, which):
        return pltpu.make_async_remote_copy(
            src_ref=send_buf.at[which * LANES + dest],
            dst_ref=landing(source, which),
            send_sem=stage_send,
            recv_sem=stage_recv.at[which],
            device_id=(z * LANES + dest, tp_here),
            device_id_type=MESH,
        )

    def spread(which):
        each(1, LANES, lambda step: stage_copy(lane, (lane + step) % LANES, which).start())
        pltpu.make_async_copy(
            send_buf.at[which * LANES + lane], landing(lane, which), stage_recv.at[which]
        ).start()

    def arrive(which):
        whole = stage_buf if which == 0 else kv_buf.at[z, (which - 1) * KEYS:which * KEYS]
        pltpu.make_async_copy(whole, whole, stage_recv.at[which]).wait()

    def weight_hop(hop):
        weight_copy(plane_at(-hop), 0).wait_recv()
        weight_copy(plane_at(-hop), 0).start()
        weight_copy(plane_at(hop), 1).wait_recv()
        weight_copy(plane_at(hop), 1).start()

    lanes = lax.broadcasted_iota(jnp.int32, (SPAN, DH), 1)
    frequency = jnp.exp((lanes % 32).astype(jnp.float32) * (-math.log(100.0) / 32))
    grid_row, grid_column = [
        jnp.broadcast_to(position_ref[axis:axis + 1, :].astype(jnp.float32), (DH, SPAN)).T
        for axis in range(2)
    ]
    angle = jnp.where(lanes < DH // 2, grid_row, grid_column) * frequency
    first = lanes % 64 < 32
    cosine = jnp.cos(angle)
    sine = jnp.sin(angle)
    sine = jnp.where(first, -sine, sine)

    def rotate(states):
        states = states.astype(jnp.float32)
        partner = jnp.where(
            first, pltpu.roll(states, DH - 32, axis=1), pltpu.roll(states, 32, axis=1)
        )
        return (states * cosine + partner * sine).astype(jnp.bfloat16)

    loads[1].wait()
    for head in range(LANES):
        send_buf[LANES + head] = rotate(key_buf[:, head * DH:(head + 1) * DH])
    loads[3].wait()

    pl.semaphore_wait(barrier, 2 + crowd - 1)
    spread(1)
    weight_copy(z, 0).start()
    weight_copy(z, 1).start()
    loads[2].wait()
    for head in range(LANES):
        send_buf[2 * LANES + head] = value_buf[:, head * DH:(head + 1) * DH]
    spread(2)
    loads[0].wait()
    for head in range(LANES):
        send_buf[head] = rotate(query_buf[:, head * DH:(head + 1) * DH])
    spread(0)

    for part in range(PARTS):
        own = segment_ref[pl.ds(z * PARTS + part, 1), :].astype(jnp.float32)
        query_segment[part * CHUNK:(part + 1) * CHUNK] = jnp.broadcast_to(own, (CHUNK, CHUNK)).T
    peak_ref[...] = jnp.full(peak_ref.shape, masked_score, jnp.float32)
    total_ref[...] = jnp.zeros(total_ref.shape, jnp.float32)
    sum_ref[...] = jnp.zeros(sum_ref.shape, jnp.float32)

    def attend(plane, chunk):
        key = kv_buf[plane, :KEYS].reshape(TOKENS, DH)
        value = kv_buf[plane, KEYS:].reshape(TOKENS, DH)
        rows = slice(chunk * CHUNK, (chunk + 1) * CHUNK)
        query = stage_buf[chunk * PER_PART:(chunk + 1) * PER_PART].reshape(CHUNK, DH)
        score = lax.dot_general(
            query, key, (((1,), (1,)), ((), ())), preferred_element_type=jnp.float32
        )
        segment = query_segment[rows]
        scores = [
            jnp.where(
                segment == segment_ref[pl.ds(plane * PARTS + part, 1), :].astype(jnp.float32),
                score[:, part * CHUNK:(part + 1) * CHUNK],
                masked_score,
            )
            for part in range(PARTS)
        ]
        top = jnp.maximum(
            jnp.maximum(scores[0], scores[1]), jnp.maximum(scores[2], scores[3])
        )
        old = peak_ref[rows]
        peak = jnp.maximum(old, jnp.max(top, axis=1, keepdims=True))
        peak_ref[rows] = peak
        fade = jnp.exp2((old - peak) * EXPONENT_SCALE)
        exponents = [jnp.exp2((part - peak) * EXPONENT_SCALE) for part in scores]
        total_ref[rows] = total_ref[rows] * fade + (
            (exponents[0] + exponents[1]) + (exponents[2] + exponents[3])
        )
        weights = jnp.concatenate([part.astype(jnp.bfloat16) for part in exponents], axis=1)
        sum_ref[rows] = sum_ref[rows] * fade + jnp.dot(
            weights, value, preferred_element_type=jnp.float32
        )

    for which in range(1, 3):
        arrive(which)
        for piece in range((which - 1) * KEYS, which * KEYS):
            ring_copy(z, piece, 0).start()
            ring_copy(z, piece, 1).start()
        weight_hop(which)
    arrive(0)
    for chunk in range(PARTS):
        attend(z, chunk)

    def quarter(step, index):
        attend(plane_at(-step if index < PARTS else step), index % PARTS)

    def quarters(step, piece):
        for index in range(piece * 2 * PARTS // PIECES, (piece + 1) * 2 * PARTS // PIECES):
            quarter(step, index)

    def ring_step(step):
        below, above = plane_at(-step), plane_at(step)
        for piece in range(PIECES):
            ring_copy(below, piece, 0).wait_recv()
            if piece < KEYS:
                ring_copy(below, piece, 0).start()
            else:
                pl.when(step < HALF_RING - 1)(lambda: ring_copy(below, piece, 0).start())
            ring_copy(above, piece, 1).wait_recv()
            if piece < KEYS:
                pl.when(step < HALF_RING - 1)(lambda: ring_copy(above, piece, 1).start())
            else:
                ring_copy(above, piece, 1).start()
            pl.when(step > 1)(lambda: quarters(step - 1, piece))
        pl.when(step % 2 == 1)(lambda: weight_hop(3 + step // 2))

    each(1, HALF_RING, ring_step)
    far = plane_at(HALF_RING)
    for piece in range(PIECES):
        ring_copy(far, piece, 0 if piece < KEYS else 1).wait_recv()
        quarters(HALF_RING - 1, piece)
    weight_copy(plane_at(-7), 0).wait_recv()
    weight_copy(plane_at(-7), 0).start()
    weight_copy(plane_at(7), 1).wait_recv()

    sibling = row * 2 + 1 - core

    def mate(step):
        return ((row + step) % GROUPS) * 2 + core

    def sibling_of(step):
        return ((row + step) % GROUPS) * 2 + 1 - core

    def plane_copy(slot, chunk, device_lane):
        return pltpu.make_async_remote_copy(
            src_ref=plane_buf.at[slot * TAIL + chunk],
            dst_ref=plane_buf.at[slot * TAIL + chunk],
            send_sem=plane_send,
            recv_sem=plane_recv.at[slot, chunk],
            device_id=(z * LANES + device_lane, tp_here),
            device_id_type=MESH,
        )

    def to_mate(step, chunk):
        return plane_copy(lane, chunk, mate(step))

    def to_sibling(step, chunk):
        return plane_copy(mate(step), chunk, sibling)

    def from_sibling(step, chunk):
        return plane_copy(sibling_of(step), chunk, lane)

    for chunk in range(TAIL):
        for quarter_index in range(chunk * PARTS // TAIL, (chunk + 1) * PARTS // TAIL):
            attend(far, quarter_index)
        rows = slice(chunk * TAIL_ROWS, (chunk + 1) * TAIL_ROWS)
        total = jnp.sum(total_ref[rows], axis=1, keepdims=True)
        plane_buf[lane * TAIL + chunk] = (sum_ref[rows] / total).astype(jnp.bfloat16)
        each(1, GROUPS, lambda step: to_mate(step, chunk).start())
        to_sibling(0, chunk).start()

    def pass_on(chunk):
        def act(step):
            to_sibling(step, chunk).wait_recv()
            to_sibling(step, chunk).start()

        each(1, GROUPS, act)

    def share_copy(source, dest):
        return pltpu.make_async_remote_copy(
            src_ref=part_buf.at[dest],
            dst_ref=share_buf.at[source],
            send_sem=share_send,
            recv_sem=share_recv,
            device_id=(z * LANES + dest % LANES, dest // LANES),
            device_id_type=MESH,
        )

    pass_on(0)
    for chunk in range(TAIL):
        if chunk + 1 < TAIL:
            pass_on(chunk + 1)
        if chunk == 0:
            weight_copy(far, 0).wait_recv()
        each(0, GROUPS, lambda step: from_sibling(step, chunk).wait_recv())
        token = jnp.concatenate([plane_buf[head * TAIL + chunk] for head in range(LANES)], axis=1)
        part = lax.dot_general(
            token,
            weight_buf[...].reshape(GROUPS * DH, LANES * DH),
            (((1,), (1,)), ((), ())),
            preferred_element_type=jnp.float32,
        ).astype(jnp.bfloat16)
        for group in range(GROUPS):
            start = group * LANES + chunk * PER_TAIL
            part_buf[start:start + PER_TAIL] = part[
                :, group * DH:(group + 1) * DH
            ].reshape(PER_TAIL, SPAN, DH)

        def share_out(step):
            dest = ((tp_here + step // PER_TAIL) % GROUPS) * LANES + chunk * PER_TAIL + step % PER_TAIL
            pl.when(dest != inside)(lambda: share_copy(inside, dest).start())

        each(0, GROUPS * PER_TAIL, share_out)

    own_share = pltpu.make_async_copy(part_buf.at[inside], share_buf.at[inside], share_recv)
    own_share.start()

    def drain(ref, sem):
        pltpu.make_async_copy(ref, ref, sem).wait()

    drain(send_buf.at[0:3 * (LANES - 1)], stage_send)
    drain(kv_buf.at[0:PLANES - 1], ring_send)
    drain(weight_buf.at[0:PLANES - 1], weight_send)
    drain(plane_buf.at[0:TAIL * (LANES - 1)], plane_send)
    loads[4].wait()
    drain(share_buf, share_recv)

    sums = []
    for source in range(LANES):
        add = share_buf[source].astype(jnp.float32)
        for group in range(1, GROUPS):
            add = add + share_buf[group * LANES + source].astype(jnp.float32)
        sums.append(add)
    for quarter in range(4):
        for half in range(2):
            projected = jnp.concatenate(
                [sums[half * 4 + i][:, quarter * 32:(quarter + 1) * 32] for i in range(4)], axis=1
            )
            columns = slice((quarter * 2 + half) * DH, (quarter * 2 + half + 1) * DH)
            encoded = residual_buf[:, columns].astype(jnp.float32) + gain_ref[:, columns] * projected
            encoded_ref[:, columns] = encoded.astype(encoded_ref.dtype)

    drain(part_buf.at[0:crowd - 1], share_send)


def local(
    query_states,
    key_states,
    value_states,
    residual,
    segment_ids,
    positions,
    out_weight,
    layer_scale,
):
    vmem = pl.BlockSpec(memory_space=pltpu.VMEM)
    hbm = pl.BlockSpec(memory_space=pltpu.HBM)
    columns, features = out_weight.shape[1], out_weight.shape[0]
    dma = pltpu.SemaphoreType.DMA
    return pl.pallas_call(
        layer_kernel,
        out_shape=pltpu.VMEM(residual.shape, jnp.bfloat16),
        in_specs=[hbm, hbm, hbm, hbm, vmem, vmem, hbm, vmem],
        out_specs=vmem,
        scratch_shapes=[
            pltpu.VMEM(query_states.shape, jnp.bfloat16),
            pltpu.VMEM(query_states.shape, jnp.bfloat16),
            pltpu.VMEM(query_states.shape, jnp.bfloat16),
            pltpu.VMEM(query_states.shape, jnp.bfloat16),
            pltpu.VMEM((3 * LANES, SPAN, DH), jnp.bfloat16),
            pltpu.VMEM((LANES, SPAN, DH), jnp.bfloat16),
            pltpu.VMEM((PLANES, PIECES, TOKENS // KEYS, DH), jnp.bfloat16),
            pltpu.VMEM((PLANES, columns, features), jnp.bfloat16),
            pltpu.VMEM((TOKENS, CHUNK), jnp.float32),
            pltpu.VMEM((TOKENS, DH), jnp.float32),
            pltpu.VMEM((TOKENS, DH), jnp.float32),
            pltpu.VMEM((TOKENS, DH), jnp.float32),
            pltpu.VMEM((LANES * TAIL, TAIL_ROWS, DH), jnp.bfloat16),
            pltpu.VMEM((GROUPS * LANES, SPAN, DH), jnp.bfloat16),
            pltpu.VMEM((GROUPS * LANES, SPAN, DH), jnp.bfloat16),
            dma(()),
            dma((3,)),
            dma(()),
            dma((PLANES, PIECES)),
            dma(()),
            dma((PLANES,)),
            dma(()),
            dma((LANES, TAIL)),
            dma(()),
            dma(()),
            dma((5,)),
        ],
        compiler_params=pltpu.CompilerParams(
            collective_id=0, has_side_effects=True, vmem_limit_bytes=56 * 1024 * 1024
        ),
    )(
        query_states,
        key_states,
        value_states,
        residual,
        segment_ids.reshape(-1, CHUNK),
        positions,
        out_weight.T,
        layer_scale[None, :],
    )


def solution(mesh):
    in_specs = (
        P("seq", "tp"),
        P("seq", "tp"),
        P("seq", "tp"),
        P("seq", "tp"),
        P(),
        P(None, "seq"),
        P("tp", "seq"),
        P("tp"),
    )
    out_specs = P("seq", "tp")
    return jax.shard_map(local, mesh=mesh, in_specs=in_specs, out_specs=out_specs, check_vma=False)
```

```python
import math

import jax
import jax.numpy as jnp
from jax import lax
from jax.experimental import pallas as pl
from jax.experimental.pallas import tpu as pltpu
from jax.sharding import PartitionSpec as P

DH = 128
PLANES = 16
LANES = 8
GROUPS = 4
SPAN = 64
TOKENS = LANES * SPAN
CHUNK = 128
HALF_RING = PLANES // 2
PIECES = 4
HALF_PIECES = PIECES // 2
SOURCES = LANES // HALF_PIECES
PARTS = TOKENS // CHUNK
PER_PART = LANES // PARTS
TAIL = 4
TAIL_ROWS = TOKENS // TAIL
PER_TAIL = LANES // TAIL
EXPONENT_SCALE = DH ** (-0.5) * math.log2(math.e)
MESH = pl.DeviceIdType.MESH

masked_score = -1e30


def each(start, stop, act):
    def body(step, carry):
        act(step)
        return carry

    lax.fori_loop(start, stop, body, 0)


def layer_kernel(
    query_ref,
    key_ref,
    value_ref,
    residual_ref,
    segment_ref,
    position_ref,
    weight_ref,
    gain_ref,
    encoded_ref,
    query_buf,
    key_buf,
    value_buf,
    residual_buf,
    send_buf,
    stage_buf,
    kv_buf,
    weight_buf,
    query_segment,
    peak_ref,
    total_ref,
    sum_ref,
    plane_buf,
    part_buf,
    share_buf,
    stage_send,
    stage_recv,
    ring_send,
    ring_recv,
    weight_send,
    weight_recv,
    plane_send,
    plane_recv,
    sibling_recv,
    share_send,
    share_recv,
    load_sem,
    peer_sem,
):
    seq_here, tp_here = lax.axis_index("seq"), lax.axis_index("tp")
    z, lane = seq_here // LANES, seq_here % LANES
    row, core = lane // 2, lane % 2
    inside = tp_here * LANES + lane
    crowd = GROUPS * LANES

    def plane_at(step):
        return (z + step + PLANES) % PLANES

    loads = [
        pltpu.make_async_copy(source, dest, load_sem.at[index])
        for index, (source, dest) in enumerate(
            [
                (query_ref, query_buf),
                (key_ref, key_buf),
                (value_ref, value_buf),
                (weight_ref, weight_buf.at[z]),
                (residual_ref, residual_buf),
            ]
        )
    ]
    for index in (2, 3, 1, 0, 4):
        loads[index].start()

    up = (plane_at(1) * LANES + lane, tp_here)
    down = (plane_at(-1) * LANES + lane, tp_here)

    barrier = pltpu.get_barrier_semaphore()

    def greet(device):
        pl.semaphore_signal(barrier, inc=1, device_id=device, device_id_type=MESH)

    greet(up)
    greet(down)

    def peer(step):
        return (seq_here, (tp_here + step) % GROUPS)

    each(1, LANES, lambda step: greet((z * LANES + (lane + step) % LANES, tp_here)))
    each(1, GROUPS, lambda step: greet(peer(step)))

    def weight_copy(plane, way):
        return pltpu.make_async_remote_copy(
            src_ref=weight_buf.at[plane],
            dst_ref=weight_buf.at[plane],
            send_sem=weight_send,
            recv_sem=weight_recv.at[plane],
            device_id=up if way == 0 else down,
            device_id_type=MESH,
        )

    def ring_copy(plane, piece, way):
        return pltpu.make_async_remote_copy(
            src_ref=kv_buf.at[plane, piece],
            dst_ref=kv_buf.at[plane, piece],
            send_sem=ring_send,
            recv_sem=ring_recv.at[plane, piece],
            device_id=up if way == 0 else down,
            device_id_type=MESH,
        )

    def landing(source, which):
        if which == 0:
            return stage_buf.at[source]
        piece = (which - 1) * HALF_PIECES + source // SOURCES
        start = pl.multiple_of(source % SOURCES * SPAN, SPAN)
        return kv_buf.at[z, piece, pl.ds(start, SPAN)]

    def stage_copy(source, dest, which):
        return pltpu.make_async_remote_copy(
            src_ref=send_buf.at[which * LANES + dest],
            dst_ref=landing(source, which),
            send_sem=stage_send,
            recv_sem=stage_recv.at[which],
            device_id=(z * LANES + dest, tp_here),
            device_id_type=MESH,
        )

    def spread(which):
        each(1, LANES, lambda step: stage_copy(lane, (lane + step) % LANES, which).start())
        pltpu.make_async_copy(
            send_buf.at[which * LANES + lane], landing(lane, which), stage_recv.at[which]
        ).start()

    def arrive(which):
        whole = stage_buf if which == 0 else kv_buf.at[z, (which - 1) * HALF_PIECES:which * HALF_PIECES]
        pltpu.make_async_copy(whole, whole, stage_recv.at[which]).wait()

    def weight_hop(hop):
        weight_copy(plane_at(-hop), 0).wait_recv()
        weight_copy(plane_at(-hop), 0).start()
        weight_copy(plane_at(hop), 1).wait_recv()
        weight_copy(plane_at(hop), 1).start()

    loads[2].wait()
    for head in range(LANES):
        send_buf[LANES + head] = value_buf[:, head * DH:(head + 1) * DH]
    loads[3].wait()

    pl.semaphore_wait(barrier, 2 + LANES - 1 + GROUPS - 1)
    spread(1)
    weight_copy(z, 0).start()
    weight_copy(z, 1).start()

    def vouch(step):
        pl.semaphore_signal(peer_sem, inc=1, device_id=peer(step), device_id_type=MESH)

    each(1, GROUPS, vouch)

    lanes = lax.broadcasted_iota(jnp.int32, (SPAN, DH), 1)
    frequency = jnp.exp((lanes % 32).astype(jnp.float32) * (-math.log(100.0) / 32))
    grid_row, grid_column = [
        jnp.broadcast_to(position_ref[axis:axis + 1, :].astype(jnp.float32), (DH, SPAN)).T
        for axis in range(2)
    ]
    angle = jnp.where(lanes < DH // 2, grid_row, grid_column) * frequency
    first = lanes % 64 < 32
    cosine = jnp.cos(angle)
    sine = jnp.sin(angle)
    sine = jnp.where(first, -sine, sine)

    def rotate(states):
        states = states.astype(jnp.float32)
        partner = jnp.where(
            first, pltpu.roll(states, DH - 32, axis=1), pltpu.roll(states, 32, axis=1)
        )
        return (states * cosine + partner * sine).astype(jnp.bfloat16)

    loads[1].wait()
    for head in range(LANES):
        send_buf[2 * LANES + head] = rotate(key_buf[:, head * DH:(head + 1) * DH])
    spread(2)
    loads[0].wait()
    for head in range(LANES):
        send_buf[head] = rotate(query_buf[:, head * DH:(head + 1) * DH])
    spread(0)

    for part in range(PARTS):
        own = segment_ref[pl.ds(z * PARTS + part, 1), :].astype(jnp.float32)
        query_segment[part * CHUNK:(part + 1) * CHUNK] = jnp.broadcast_to(own, (CHUNK, CHUNK)).T
    peak_ref[...] = jnp.full(peak_ref.shape, masked_score, jnp.float32)
    total_ref[...] = jnp.zeros(total_ref.shape, jnp.float32)
    sum_ref[...] = jnp.zeros(sum_ref.shape, jnp.float32)

    def attend(plane, chunk):
        value = kv_buf[plane, :HALF_PIECES].reshape(TOKENS, DH)
        key = kv_buf[plane, HALF_PIECES:].reshape(TOKENS, DH)
        rows = slice(chunk * CHUNK, (chunk + 1) * CHUNK)
        query = stage_buf[chunk * PER_PART:(chunk + 1) * PER_PART].reshape(CHUNK, DH)
        score = lax.dot_general(
            query, key, (((1,), (1,)), ((), ())), preferred_element_type=jnp.float32
        )
        segment = query_segment[rows]
        scores = [
            jnp.where(
                segment == segment_ref[pl.ds(plane * PARTS + part, 1), :].astype(jnp.float32),
                score[:, part * CHUNK:(part + 1) * CHUNK],
                masked_score,
            )
            for part in range(PARTS)
        ]
        top = jnp.maximum(
            jnp.maximum(scores[0], scores[1]), jnp.maximum(scores[2], scores[3])
        )
        old = peak_ref[rows]
        peak = jnp.maximum(old, jnp.max(top, axis=1, keepdims=True))
        peak_ref[rows] = peak
        fade = jnp.exp2((old - peak) * EXPONENT_SCALE)
        exponents = [jnp.exp2((part - peak) * EXPONENT_SCALE) for part in scores]
        total_ref[rows] = total_ref[rows] * fade + (
            (exponents[0] + exponents[1]) + (exponents[2] + exponents[3])
        )
        weights = jnp.concatenate([part.astype(jnp.bfloat16) for part in exponents], axis=1)
        sum_ref[rows] = sum_ref[rows] * fade + jnp.dot(
            weights, value, preferred_element_type=jnp.float32
        )

    for which in range(1, 3):
        arrive(which)
        for piece in range((which - 1) * HALF_PIECES, which * HALF_PIECES):
            ring_copy(z, piece, 0).start()
            ring_copy(z, piece, 1).start()
    weight_hop(1)
    arrive(0)
    for chunk in range(PARTS):
        attend(z, chunk)

    def quarter(step, index):
        attend(plane_at(-step if index < PARTS else step), index % PARTS)

    def quarters(step, piece):
        for index in range(piece * 2 * PARTS // PIECES, (piece + 1) * 2 * PARTS // PIECES):
            quarter(step, index)

    def ring_step(step):
        below, above = plane_at(-step), plane_at(step)
        for piece in range(PIECES):
            ring_copy(below, piece, 0).wait_recv()
            if piece < HALF_PIECES:
                ring_copy(below, piece, 0).start()
            else:
                pl.when(step < HALF_RING - 1)(lambda: ring_copy(below, piece, 0).start())
            ring_copy(above, piece, 1).wait_recv()
            if piece < HALF_PIECES:
                pl.when(step < HALF_RING - 1)(lambda: ring_copy(above, piece, 1).start())
            else:
                ring_copy(above, piece, 1).start()
            pl.when(step > 1)(lambda: quarters(step - 1, piece))
        pl.when(step % 3 != 0)(lambda: weight_hop(step + 1 - step // 3))

    each(1, HALF_RING, ring_step)
    far = plane_at(HALF_RING)
    for piece in range(PIECES):
        ring_copy(far, piece, 0 if piece < HALF_PIECES else 1).wait_recv()
        quarters(HALF_RING - 1, piece)
    weight_copy(plane_at(-7), 0).wait_recv()
    weight_copy(plane_at(-7), 0).start()
    weight_copy(plane_at(7), 1).wait_recv()

    sibling = row * 2 + 1 - core

    def mate(step):
        return ((row + step) % GROUPS) * 2 + core

    def plane_copy(slot, chunk, device_lane, recv_sem):
        return pltpu.make_async_remote_copy(
            src_ref=plane_buf.at[slot * TAIL + chunk],
            dst_ref=plane_buf.at[slot * TAIL + chunk],
            send_sem=plane_send,
            recv_sem=recv_sem,
            device_id=(z * LANES + device_lane, tp_here),
            device_id_type=MESH,
        )

    def to_mate(step, chunk):
        return plane_copy(lane, chunk, mate(step), plane_recv.at[row, chunk])

    def to_sibling(step, chunk):
        return plane_copy(mate(step), chunk, sibling, sibling_recv.at[chunk])

    def from_mate(step, chunk):
        return plane_copy(mate(step), chunk, lane, plane_recv.at[(row + step) % GROUPS, chunk])

    for chunk in range(TAIL):
        for quarter_index in range(chunk * PARTS // TAIL, (chunk + 1) * PARTS // TAIL):
            attend(far, quarter_index)
        rows = slice(chunk * TAIL_ROWS, (chunk + 1) * TAIL_ROWS)
        total = jnp.sum(total_ref[rows], axis=1, keepdims=True)
        plane_buf[lane * TAIL + chunk] = (sum_ref[rows] / total).astype(jnp.bfloat16)
        each(1, GROUPS, lambda step: to_mate(step, chunk).start())
        to_sibling(0, chunk).start()

    def pass_on(chunk):
        def act(step):
            from_mate(step, chunk).wait_recv()
            to_sibling(step, chunk).start()

        each(1, GROUPS, act)

    def share_copy(source, dest):
        return pltpu.make_async_remote_copy(
            src_ref=part_buf.at[dest],
            dst_ref=share_buf.at[source],
            send_sem=share_send,
            recv_sem=share_recv,
            device_id=(z * LANES + dest % LANES, dest // LANES),
            device_id_type=MESH,
        )

    pl.semaphore_wait(peer_sem, GROUPS - 1)
    def drain(ref, sem):
        pltpu.make_async_copy(ref, ref, sem).wait()

    pass_on(0)
    for chunk in range(TAIL):
        if chunk + 1 < TAIL:
            pass_on(chunk + 1)
        if chunk == 0:
            weight_copy(far, 0).wait_recv()
        drain(plane_buf.at[0:GROUPS], sibling_recv.at[chunk])
        token = jnp.concatenate([plane_buf[head * TAIL + chunk] for head in range(LANES)], axis=1)
        part = lax.dot_general(
            token,
            weight_buf[...].reshape(GROUPS * DH, LANES * DH),
            (((1,), (1,)), ((), ())),
            preferred_element_type=jnp.float32,
        ).astype(jnp.bfloat16)
        for group in range(GROUPS):
            start = group * LANES + chunk * PER_TAIL
            part_buf[start:start + PER_TAIL] = part[
                :, group * DH:(group + 1) * DH
            ].reshape(PER_TAIL, SPAN, DH)

        def share_out(step):
            dest = ((tp_here + step // PER_TAIL) % GROUPS) * LANES + chunk * PER_TAIL + step % PER_TAIL
            pl.when(dest != inside)(lambda: share_copy(inside, dest).start())

        each(0, GROUPS * PER_TAIL, share_out)

    own_share = pltpu.make_async_copy(part_buf.at[inside], share_buf.at[inside], share_recv)
    own_share.start()

    drain(send_buf.at[0:3 * (LANES - 1)], stage_send)
    drain(kv_buf.at[0:PLANES - 1], ring_send)
    drain(weight_buf.at[0:PLANES - 1], weight_send)
    drain(plane_buf.at[0:TAIL * (LANES - 1)], plane_send)
    loads[4].wait()
    drain(share_buf, share_recv)

    sums = []
    for source in range(LANES):
        add = share_buf[source].astype(jnp.float32)
        for group in range(1, GROUPS):
            add = add + share_buf[group * LANES + source].astype(jnp.float32)
        sums.append(add)
    for quarter in range(4):
        for half in range(2):
            projected = jnp.concatenate(
                [sums[half * 4 + i][:, quarter * 32:(quarter + 1) * 32] for i in range(4)], axis=1
            )
            columns = slice((quarter * 2 + half) * DH, (quarter * 2 + half + 1) * DH)
            encoded = residual_buf[:, columns].astype(jnp.float32) + gain_ref[:, columns] * projected
            encoded_ref[:, columns] = encoded.astype(encoded_ref.dtype)

    drain(part_buf.at[0:crowd - 1], share_send)


def local(
    query_states,
    key_states,
    value_states,
    residual,
    segment_ids,
    positions,
    out_weight,
    layer_scale,
):
    vmem = pl.BlockSpec(memory_space=pltpu.VMEM)
    hbm = pl.BlockSpec(memory_space=pltpu.HBM)
    columns, features = out_weight.shape[1], out_weight.shape[0]
    dma = pltpu.SemaphoreType.DMA
    return pl.pallas_call(
        layer_kernel,
        out_shape=pltpu.VMEM(residual.shape, jnp.bfloat16),
        in_specs=[hbm, hbm, hbm, hbm, vmem, vmem, hbm, vmem],
        out_specs=vmem,
        scratch_shapes=[
            pltpu.VMEM(query_states.shape, jnp.bfloat16),
            pltpu.VMEM(query_states.shape, jnp.bfloat16),
            pltpu.VMEM(query_states.shape, jnp.bfloat16),
            pltpu.VMEM(query_states.shape, jnp.bfloat16),
            pltpu.VMEM((3 * LANES, SPAN, DH), jnp.bfloat16),
            pltpu.VMEM((LANES, SPAN, DH), jnp.bfloat16),
            pltpu.VMEM((PLANES, PIECES, TOKENS // HALF_PIECES, DH), jnp.bfloat16),
            pltpu.VMEM((PLANES, columns, features), jnp.bfloat16),
            pltpu.VMEM((TOKENS, CHUNK), jnp.float32),
            pltpu.VMEM((TOKENS, DH), jnp.float32),
            pltpu.VMEM((TOKENS, DH), jnp.float32),
            pltpu.VMEM((TOKENS, DH), jnp.float32),
            pltpu.VMEM((LANES * TAIL, TAIL_ROWS, DH), jnp.bfloat16),
            pltpu.VMEM((GROUPS * LANES, SPAN, DH), jnp.bfloat16),
            pltpu.VMEM((GROUPS * LANES, SPAN, DH), jnp.bfloat16),
            dma(()),
            dma((3,)),
            dma(()),
            dma((PLANES, PIECES)),
            dma(()),
            dma((PLANES,)),
            dma(()),
            dma((GROUPS, TAIL)),
            dma((TAIL,)),
            dma(()),
            dma(()),
            dma((5,)),
            pltpu.SemaphoreType.REGULAR,
        ],
        compiler_params=pltpu.CompilerParams(
            collective_id=0, has_side_effects=True, vmem_limit_bytes=56 * 1024 * 1024
        ),
    )(
        query_states,
        key_states,
        value_states,
        residual,
        segment_ids.reshape(-1, CHUNK),
        positions,
        out_weight.T,
        layer_scale[None, :],
    )


def solution(mesh):
    in_specs = (
        P("seq", "tp"),
        P("seq", "tp"),
        P("seq", "tp"),
        P("seq", "tp"),
        P(),
        P(None, "seq"),
        P("tp", "seq"),
        P("tp"),
    )
    out_specs = P("seq", "tp")
    return jax.shard_map(local, mesh=mesh, in_specs=in_specs, out_specs=out_specs, check_vma=False)
```

```python
import math

import jax
import jax.numpy as jnp
from jax import lax
from jax.experimental import pallas as pl
from jax.experimental.pallas import tpu as pltpu
from jax.sharding import PartitionSpec as P

DH = 128
PLANES = 16
LANES = 8
GROUPS = 4
SPAN = 64
TOKENS = LANES * SPAN
CHUNK = 128
HALF_RING = PLANES // 2
PIECES = 2
HALF_PIECES = PIECES // 2
SOURCES = LANES // HALF_PIECES
PARTS = TOKENS // CHUNK
PER_PART = LANES // PARTS
TAIL = 4
TAIL_ROWS = TOKENS // TAIL
PER_TAIL = LANES // TAIL
EXPONENT_SCALE = DH ** (-0.5) * math.log2(math.e)
MESH = pl.DeviceIdType.MESH

masked_score = -1e30


def each(start, stop, act):
    def body(step, carry):
        act(step)
        return carry

    lax.fori_loop(start, stop, body, 0)


def layer_kernel(
    query_ref,
    key_ref,
    value_ref,
    residual_ref,
    segment_ref,
    position_ref,
    weight_ref,
    gain_ref,
    encoded_ref,
    query_buf,
    key_buf,
    value_buf,
    residual_buf,
    send_buf,
    stage_buf,
    kv_buf,
    weight_buf,
    query_segment,
    peak_ref,
    total_ref,
    sum_ref,
    plane_buf,
    part_buf,
    share_buf,
    stage_send,
    stage_recv,
    ring_send,
    ring_recv,
    weight_send,
    weight_recv,
    plane_send,
    plane_recv,
    sibling_recv,
    share_send,
    share_recv,
    load_sem,
    peer_sem,
):
    seq_here, tp_here = lax.axis_index("seq"), lax.axis_index("tp")
    z, lane = seq_here // LANES, seq_here % LANES
    row, core = lane // 2, lane % 2
    inside = tp_here * LANES + lane
    crowd = GROUPS * LANES

    def plane_at(step):
        return (z + step + PLANES) % PLANES

    loads = [
        pltpu.make_async_copy(source, dest, load_sem.at[index])
        for index, (source, dest) in enumerate(
            [
                (query_ref, query_buf),
                (key_ref, key_buf),
                (value_ref, value_buf),
                (weight_ref, weight_buf.at[z]),
                (residual_ref, residual_buf),
            ]
        )
    ]
    for index in (2, 3, 1, 0, 4):
        loads[index].start()

    up = (plane_at(1) * LANES + lane, tp_here)
    down = (plane_at(-1) * LANES + lane, tp_here)

    barrier = pltpu.get_barrier_semaphore()

    def greet(device):
        pl.semaphore_signal(barrier, inc=1, device_id=device, device_id_type=MESH)

    greet(up)
    greet(down)

    def peer(step):
        return (seq_here, (tp_here + step) % GROUPS)

    each(1, LANES, lambda step: greet((z * LANES + (lane + step) % LANES, tp_here)))
    each(1, GROUPS, lambda step: greet(peer(step)))

    def weight_copy(plane, way):
        return pltpu.make_async_remote_copy(
            src_ref=weight_buf.at[plane],
            dst_ref=weight_buf.at[plane],
            send_sem=weight_send,
            recv_sem=weight_recv.at[plane],
            device_id=up if way == 0 else down,
            device_id_type=MESH,
        )

    def ring_copy(plane, piece, way):
        return pltpu.make_async_remote_copy(
            src_ref=kv_buf.at[plane, piece],
            dst_ref=kv_buf.at[plane, piece],
            send_sem=ring_send,
            recv_sem=ring_recv.at[plane, piece],
            device_id=up if way == 0 else down,
            device_id_type=MESH,
        )

    def landing(source, which):
        if which == 0:
            return stage_buf.at[source]
        piece = (which - 1) * HALF_PIECES + source // SOURCES
        start = pl.multiple_of(source % SOURCES * SPAN, SPAN)
        return kv_buf.at[z, piece, pl.ds(start, SPAN)]

    def stage_copy(source, dest, which):
        return pltpu.make_async_remote_copy(
            src_ref=send_buf.at[which * LANES + dest],
            dst_ref=landing(source, which),
            send_sem=stage_send,
            recv_sem=stage_recv.at[which],
            device_id=(z * LANES + dest, tp_here),
            device_id_type=MESH,
        )

    def spread(which):
        each(1, LANES, lambda step: stage_copy(lane, (lane + step) % LANES, which).start())
        pltpu.make_async_copy(
            send_buf.at[which * LANES + lane], landing(lane, which), stage_recv.at[which]
        ).start()

    def arrive(which):
        whole = stage_buf if which == 0 else kv_buf.at[z, (which - 1) * HALF_PIECES:which * HALF_PIECES]
        pltpu.make_async_copy(whole, whole, stage_recv.at[which]).wait()

    def weight_hop(hop):
        weight_copy(plane_at(-hop), 0).wait_recv()
        weight_copy(plane_at(-hop), 0).start()
        weight_copy(plane_at(hop), 1).wait_recv()
        weight_copy(plane_at(hop), 1).start()

    loads[2].wait()
    for head in range(LANES):
        send_buf[LANES + head] = value_buf[:, head * DH:(head + 1) * DH]
    loads[3].wait()

    pl.semaphore_wait(barrier, 2 + LANES - 1 + GROUPS - 1)
    spread(1)
    weight_copy(z, 0).start()
    weight_copy(z, 1).start()

    def vouch(step):
        pl.semaphore_signal(peer_sem, inc=1, device_id=peer(step), device_id_type=MESH)

    each(1, GROUPS, vouch)

    lanes = lax.broadcasted_iota(jnp.int32, (SPAN, DH), 1)
    frequency = jnp.exp((lanes % 32).astype(jnp.float32) * (-math.log(100.0) / 32))
    grid_row, grid_column = [
        jnp.broadcast_to(position_ref[axis:axis + 1, :].astype(jnp.float32), (DH, SPAN)).T
        for axis in range(2)
    ]
    angle = jnp.where(lanes < DH // 2, grid_row, grid_column) * frequency
    first = lanes % 64 < 32
    cosine = jnp.cos(angle)
    sine = jnp.sin(angle)
    sine = jnp.where(first, -sine, sine)

    def rotate(states):
        states = states.astype(jnp.float32)
        partner = jnp.where(
            first, pltpu.roll(states, DH - 32, axis=1), pltpu.roll(states, 32, axis=1)
        )
        return (states * cosine + partner * sine).astype(jnp.bfloat16)

    loads[1].wait()
    for head in range(LANES):
        send_buf[2 * LANES + head] = rotate(key_buf[:, head * DH:(head + 1) * DH])
    spread(2)
    loads[0].wait()
    for head in range(LANES):
        send_buf[head] = rotate(query_buf[:, head * DH:(head + 1) * DH])
    spread(0)

    for part in range(PARTS):
        own = segment_ref[pl.ds(z * PARTS + part, 1), :].astype(jnp.float32)
        query_segment[part * CHUNK:(part + 1) * CHUNK] = jnp.broadcast_to(own, (CHUNK, CHUNK)).T
    peak_ref[...] = jnp.full(peak_ref.shape, masked_score, jnp.float32)
    total_ref[...] = jnp.zeros(total_ref.shape, jnp.float32)
    sum_ref[...] = jnp.zeros(sum_ref.shape, jnp.float32)

    def attend(plane, chunk):
        value = kv_buf[plane, :HALF_PIECES].reshape(TOKENS, DH)
        key = kv_buf[plane, HALF_PIECES:].reshape(TOKENS, DH)
        rows = slice(chunk * CHUNK, (chunk + 1) * CHUNK)
        query = stage_buf[chunk * PER_PART:(chunk + 1) * PER_PART].reshape(CHUNK, DH)
        score = lax.dot_general(
            query, key, (((1,), (1,)), ((), ())), preferred_element_type=jnp.float32
        )
        segment = query_segment[rows]
        scores = [
            jnp.where(
                segment == segment_ref[pl.ds(plane * PARTS + part, 1), :].astype(jnp.float32),
                score[:, part * CHUNK:(part + 1) * CHUNK],
                masked_score,
            )
            for part in range(PARTS)
        ]
        top = jnp.maximum(
            jnp.maximum(scores[0], scores[1]), jnp.maximum(scores[2], scores[3])
        )
        old = peak_ref[rows]
        peak = jnp.maximum(old, jnp.max(top, axis=1, keepdims=True))
        peak_ref[rows] = peak
        fade = jnp.exp2((old - peak) * EXPONENT_SCALE)
        exponents = [jnp.exp2((part - peak) * EXPONENT_SCALE) for part in scores]
        total_ref[rows] = total_ref[rows] * fade + (
            (exponents[0] + exponents[1]) + (exponents[2] + exponents[3])
        )
        weights = jnp.concatenate([part.astype(jnp.bfloat16) for part in exponents], axis=1)
        sum_ref[rows] = sum_ref[rows] * fade + jnp.dot(
            weights, value, preferred_element_type=jnp.float32
        )

    for which in range(1, 3):
        arrive(which)
        for piece in range((which - 1) * HALF_PIECES, which * HALF_PIECES):
            ring_copy(z, piece, 0).start()
            ring_copy(z, piece, 1).start()
    weight_hop(1)
    arrive(0)
    for chunk in range(PARTS):
        attend(z, chunk)

    def quarter(step, index):
        attend(plane_at(-step if index < PARTS else step), index % PARTS)

    def quarters(step, piece):
        for index in range(piece * 2 * PARTS // PIECES, (piece + 1) * 2 * PARTS // PIECES):
            quarter(step, index)

    def ring_step(step):
        below, above = plane_at(-step), plane_at(step)
        for piece in range(PIECES):
            ring_copy(below, piece, 0).wait_recv()
            if piece < HALF_PIECES:
                ring_copy(below, piece, 0).start()
            else:
                pl.when(step < HALF_RING - 1)(lambda: ring_copy(below, piece, 0).start())
            ring_copy(above, piece, 1).wait_recv()
            if piece < HALF_PIECES:
                pl.when(step < HALF_RING - 1)(lambda: ring_copy(above, piece, 1).start())
            else:
                ring_copy(above, piece, 1).start()
            pl.when(step > 1)(lambda: quarters(step - 1, piece))
        pl.when(step % 3 != 0)(lambda: weight_hop(step + 1 - step // 3))

    each(1, HALF_RING, ring_step)
    far = plane_at(HALF_RING)
    for piece in range(PIECES):
        ring_copy(far, piece, 0 if piece < HALF_PIECES else 1).wait_recv()
        quarters(HALF_RING - 1, piece)
    weight_copy(plane_at(-7), 0).wait_recv()
    weight_copy(plane_at(-7), 0).start()
    weight_copy(plane_at(7), 1).wait_recv()

    sibling = row * 2 + 1 - core

    def mate(step):
        return ((row + step) % GROUPS) * 2 + core

    def plane_copy(slot, chunk, device_lane, recv_sem):
        return pltpu.make_async_remote_copy(
            src_ref=plane_buf.at[slot * TAIL + chunk],
            dst_ref=plane_buf.at[slot * TAIL + chunk],
            send_sem=plane_send,
            recv_sem=recv_sem,
            device_id=(z * LANES + device_lane, tp_here),
            device_id_type=MESH,
        )

    def to_mate(step, chunk):
        return plane_copy(lane, chunk, mate(step), plane_recv.at[row, chunk])

    def to_sibling(step, chunk):
        return plane_copy(mate(step), chunk, sibling, sibling_recv.at[chunk])

    def from_mate(step, chunk):
        return plane_copy(mate(step), chunk, lane, plane_recv.at[(row + step) % GROUPS, chunk])

    for chunk in range(TAIL):
        for quarter_index in range(chunk * PARTS // TAIL, (chunk + 1) * PARTS // TAIL):
            attend(far, quarter_index)
        rows = slice(chunk * TAIL_ROWS, (chunk + 1) * TAIL_ROWS)
        total = jnp.sum(total_ref[rows], axis=1, keepdims=True)
        plane_buf[lane * TAIL + chunk] = (sum_ref[rows] / total).astype(jnp.bfloat16)
        each(1, GROUPS, lambda step: to_mate(step, chunk).start())
        to_sibling(0, chunk).start()

    def pass_on(chunk):
        def act(step):
            from_mate(step, chunk).wait_recv()
            to_sibling(step, chunk).start()

        each(1, GROUPS, act)

    def share_copy(source, dest):
        return pltpu.make_async_remote_copy(
            src_ref=part_buf.at[dest],
            dst_ref=share_buf.at[source],
            send_sem=share_send,
            recv_sem=share_recv,
            device_id=(z * LANES + dest % LANES, dest // LANES),
            device_id_type=MESH,
        )

    pl.semaphore_wait(peer_sem, GROUPS - 1)
    def drain(ref, sem):
        pltpu.make_async_copy(ref, ref, sem).wait()

    pass_on(0)
    for chunk in range(TAIL):
        if chunk + 1 < TAIL:
            pass_on(chunk + 1)
        if chunk == 0:
            weight_copy(far, 0).wait_recv()
        drain(plane_buf.at[0:GROUPS], sibling_recv.at[chunk])
        token = jnp.concatenate([plane_buf[head * TAIL + chunk] for head in range(LANES)], axis=1)
        part = lax.dot_general(
            token,
            weight_buf[...].reshape(GROUPS * DH, LANES * DH),
            (((1,), (1,)), ((), ())),
            preferred_element_type=jnp.float32,
        ).astype(jnp.bfloat16)
        for group in range(GROUPS):
            start = group * LANES + chunk * PER_TAIL
            part_buf[start:start + PER_TAIL] = part[
                :, group * DH:(group + 1) * DH
            ].reshape(PER_TAIL, SPAN, DH)

        def share_out(step):
            dest = ((tp_here + step // PER_TAIL) % GROUPS) * LANES + chunk * PER_TAIL + step % PER_TAIL
            pl.when(dest != inside)(lambda: share_copy(inside, dest).start())

        each(0, GROUPS * PER_TAIL, share_out)

    own_share = pltpu.make_async_copy(part_buf.at[inside], share_buf.at[inside], share_recv)
    own_share.start()

    drain(send_buf.at[0:3 * (LANES - 1)], stage_send)
    drain(kv_buf.at[0:PLANES - 1], ring_send)
    drain(weight_buf.at[0:PLANES - 1], weight_send)
    drain(plane_buf.at[0:TAIL * (LANES - 1)], plane_send)
    loads[4].wait()
    drain(share_buf, share_recv)

    sums = []
    for source in range(LANES):
        add = share_buf[source].astype(jnp.float32)
        for group in range(1, GROUPS):
            add = add + share_buf[group * LANES + source].astype(jnp.float32)
        sums.append(add)
    for quarter in range(4):
        for half in range(2):
            projected = jnp.concatenate(
                [sums[half * 4 + i][:, quarter * 32:(quarter + 1) * 32] for i in range(4)], axis=1
            )
            columns = slice((quarter * 2 + half) * DH, (quarter * 2 + half + 1) * DH)
            encoded = residual_buf[:, columns].astype(jnp.float32) + gain_ref[:, columns] * projected
            encoded_ref[:, columns] = encoded.astype(encoded_ref.dtype)

    drain(part_buf.at[0:crowd - 1], share_send)


def local(
    query_states,
    key_states,
    value_states,
    residual,
    segment_ids,
    positions,
    out_weight,
    layer_scale,
):
    vmem = pl.BlockSpec(memory_space=pltpu.VMEM)
    hbm = pl.BlockSpec(memory_space=pltpu.HBM)
    columns, features = out_weight.shape[1], out_weight.shape[0]
    dma = pltpu.SemaphoreType.DMA
    return pl.pallas_call(
        layer_kernel,
        out_shape=pltpu.VMEM(residual.shape, jnp.bfloat16),
        in_specs=[hbm, hbm, hbm, hbm, vmem, vmem, hbm, vmem],
        out_specs=vmem,
        scratch_shapes=[
            pltpu.VMEM(query_states.shape, jnp.bfloat16),
            pltpu.VMEM(query_states.shape, jnp.bfloat16),
            pltpu.VMEM(query_states.shape, jnp.bfloat16),
            pltpu.VMEM(query_states.shape, jnp.bfloat16),
            pltpu.VMEM((3 * LANES, SPAN, DH), jnp.bfloat16),
            pltpu.VMEM((LANES, SPAN, DH), jnp.bfloat16),
            pltpu.VMEM((PLANES, PIECES, TOKENS // HALF_PIECES, DH), jnp.bfloat16),
            pltpu.VMEM((PLANES, columns, features), jnp.bfloat16),
            pltpu.VMEM((TOKENS, CHUNK), jnp.float32),
            pltpu.VMEM((TOKENS, DH), jnp.float32),
            pltpu.VMEM((TOKENS, DH), jnp.float32),
            pltpu.VMEM((TOKENS, DH), jnp.float32),
            pltpu.VMEM((LANES * TAIL, TAIL_ROWS, DH), jnp.bfloat16),
            pltpu.VMEM((GROUPS * LANES, SPAN, DH), jnp.bfloat16),
            pltpu.VMEM((GROUPS * LANES, SPAN, DH), jnp.bfloat16),
            dma(()),
            dma((3,)),
            dma(()),
            dma((PLANES, PIECES)),
            dma(()),
            dma((PLANES,)),
            dma(()),
            dma((GROUPS, TAIL)),
            dma((TAIL,)),
            dma(()),
            dma(()),
            dma((5,)),
            pltpu.SemaphoreType.REGULAR,
        ],
        compiler_params=pltpu.CompilerParams(
            collective_id=0, has_side_effects=True, vmem_limit_bytes=56 * 1024 * 1024
        ),
    )(
        query_states,
        key_states,
        value_states,
        residual,
        segment_ids.reshape(-1, CHUNK),
        positions,
        out_weight.T,
        layer_scale[None, :],
    )


def solution(mesh):
    in_specs = (
        P("seq", "tp"),
        P("seq", "tp"),
        P("seq", "tp"),
        P("seq", "tp"),
        P(),
        P(None, "seq"),
        P("tp", "seq"),
        P("tp"),
    )
    out_specs = P("seq", "tp")
    return jax.shard_map(local, mesh=mesh, in_specs=in_specs, out_specs=out_specs, check_vma=False)
```
